128 devices in a mesh: wide: 64 (over y, z_lo, x, core), narrow: 2 (over z_hi).
Axes of the slice: x: 4, y: 4, z: 4 (z_hi: 2, z_lo: 2; z = z_hi * 2 + z_lo), core: 2. Of those that a mesh axis runs over, the one named last changes fastest.
Arguments:
- voltages: bfloat16 [512, 1048576], P('wide', 'narrow'), may hold values from -6 to 6
- following: bfloat16 [512, 30720], P('wide'), may hold values from -6 to 6
Outputs:
- visibilities: float32 [1024, 2, 512, 512], P(('wide', 'narrow'))
The draws below stay inside these ranges and needn't reach their ends.
All inputs are finite; a program needn't handle non-finite values.
Results may differ from the reference program's by a relative error of at most 0.0028.
Values may be sent and summed in bfloat16 or wider, within the bound.
A program may use at most 192 MiB of HBM per device.

```python
import math
import jax
import jax.numpy as jnp
from jax import lax

FFT_LEN = 2048
CHANNELS = 1024
TAPS = 16
INPUTS = 512
SPECTRA = 512
SAMPLES = 1048576


def shard_levels(stream_key, dims, shards, smallest, high):
    loudness = 1.0
    for axis_at, blocks in shards:
        steps = jax.random.uniform(jax.random.fold_in(jax.random.fold_in(stream_key, 6), axis_at), (blocks,), jnp.float32, smallest / len(shards), high / len(shards))
        loudness = loudness * jnp.repeat(jnp.exp(steps), dims[axis_at] // blocks).reshape((-1,) + (1,) * (len(dims) - 1 - axis_at))
    return loudness


def bell_draw(key, extent, scale, bound, shards=(), held_as=jnp.bfloat16):
    array = jax.random.normal(key, extent, jnp.float32) * scale
    if len(shards) > 0:
        array = shard_levels(key, extent, shards, -0.22, 0.18) * array
    return jnp.clip(array, min=-bound, max=bound).astype(held_as)


def setup_inputs(seed: int = 0) -> dict:
    key_list = jax.random.split(jax.random.key(seed), 3)
    return {
        "voltages": bell_draw(key_list[0], (INPUTS, SAMPLES), 1.0, 6.0, ((0, 64), (1, 2))),
        "following": bell_draw(key_list[1], (INPUTS, (TAPS - 1) * FFT_LEN), 1.0, 6.0, ((0, 64),)),
    }


def pfb_window(block_len, tap_count):
    length_all = tap_count * block_len
    sample_pos = jnp.arange(length_all, dtype=jnp.float32)
    centred = (sample_pos + 0.5 - length_all / 2.0) / block_len
    taper = 0.5 - 0.5 * jnp.cos(2.0 * jnp.pi * (sample_pos + 0.5) / length_all)
    return jnp.sinc(centred) * taper

def reference(voltages, following):
    weights_taps = pfb_window(FFT_LEN, TAPS).reshape(TAPS, FFT_LEN)
    extended = jnp.concatenate([voltages, following], axis=1)
    scaling = 1.0 / math.sqrt(FFT_LEN)

    def one_input(series):
        blocks = series.astype(jnp.float32).reshape(SPECTRA + TAPS - 1, FFT_LEN)
        filtered = jnp.zeros((SPECTRA, FFT_LEN), jnp.float32)
        for tap_index in range(TAPS):
            filtered = filtered + weights_taps[tap_index][None, :] * blocks[tap_index:tap_index + SPECTRA]
        spectrum = jnp.fft.rfft(filtered, axis=-1)[:, :CHANNELS] * scaling
        return (jnp.real(spectrum).astype(jnp.bfloat16), jnp.imag(spectrum).astype(jnp.bfloat16))
    real_part, imag_part = lax.map(one_input, extended)
    half = INPUTS

    def channel_block(first):
        real_block = lax.dynamic_slice_in_dim(real_part, first, 8, 2)
        imag_block = lax.dynamic_slice_in_dim(imag_part, first, 8, 2)
        stacked = jnp.concatenate([real_block, imag_block], axis=0).astype(jnp.float32)
        gram = jnp.einsum('isc,jsc->cij', stacked, stacked, precision=lax.Precision.HIGHEST)
        vis_real = gram[:, :half, :half] + gram[:, half:, half:]
        vis_imag = gram[:, half:, :half] - gram[:, :half, half:]
        return jnp.stack([vis_real, vis_imag], axis=1) / SPECTRA
    starts = (jnp.arange(CHANNELS // 8) * 8).astype(jnp.int32)
    result = lax.map(channel_block, starts)
    return result.reshape(CHANNELS, 2, INPUTS, INPUTS)
```

```python
import math

import jax
import jax.numpy as jnp
from jax import lax
from jax.sharding import PartitionSpec as P

FFT_LEN = 2048
CHANNELS = 1024
TAPS = 16


def from_behind(x, axis, by):
    size = lax.axis_size(axis)
    pairs = [(i, i + by) for i in range(size) if 0 <= i + by < size]
    return lax.ppermute(x, axis, pairs)


def pfb_window(block_len, tap_count):
    length_all = tap_count * block_len
    sample_pos = jnp.arange(length_all, dtype=jnp.float32)
    centred = (sample_pos + 0.5 - length_all / 2.0) / block_len
    taper = 0.5 - 0.5 * jnp.cos(2.0 * jnp.pi * (sample_pos + 0.5) / length_all)
    return jnp.sinc(centred) * taper


def phase(first_idx, second_idx):
    turns = (first_idx * second_idx % FFT_LEN).astype(jnp.float32)
    angles = (2.0 * jnp.pi / FFT_LEN) * turns
    return jnp.cos(angles), jnp.sin(angles)


def dft_matrix(salt):
    chan = jnp.arange(CHANNELS, dtype=jnp.int32)[None, :] + salt
    hi_c, hi_s = phase(jnp.arange(FFT_LEN // 64, dtype=jnp.int32)[:, None] * 64, chan)
    lo_c, lo_s = phase(jnp.arange(64, dtype=jnp.int32)[:, None], chan)
    cos_t = hi_c[:, None, :] * lo_c[None, :, :] - hi_s[:, None, :] * lo_s[None, :, :]
    sin_t = hi_s[:, None, :] * lo_c[None, :, :] + hi_c[:, None, :] * lo_s[None, :, :]
    scaling = 1.0 / math.sqrt(FFT_LEN)
    table = jnp.concatenate([cos_t * scaling, sin_t * (-scaling)], axis=-1)
    return table.reshape(FFT_LEN, 2 * CHANNELS)


def shards(voltages, following):
    local_inputs, local_span = voltages.shape
    local_spec = local_span // FFT_LEN
    halo_len = (TAPS - 1) * FFT_LEN
    leading = voltages[:, :halo_len]
    shifted = from_behind(leading, "narrow", -1)
    is_final = lax.axis_index("narrow") == lax.axis_size("narrow") - 1
    after_rows = jnp.where(is_final, following, shifted)
    samples = jnp.concatenate([voltages, after_rows], axis=1)
    blocks = samples.reshape(local_inputs, local_spec + TAPS - 1, FFT_LEN).astype(jnp.float32)
    weights_taps = pfb_window(FFT_LEN, TAPS).reshape(TAPS, FFT_LEN)
    filtered = weights_taps[0][None, None, :] * blocks[:, 0:local_spec, :]
    for tap_index in range(1, TAPS):
        filtered = filtered + weights_taps[tap_index][None, None, :] * blocks[
            :, tap_index : tap_index + local_spec, :
        ]
    salt = lax.optimization_barrier(jnp.zeros((), jnp.int32))
    table = dft_matrix(salt)
    rows = filtered.reshape(local_inputs * local_spec, FFT_LEN)
    spec = jnp.einsum("rk,kn->nr", rows, table, precision=lax.Precision.HIGH,
                      preferred_element_type=jnp.float32)
    spec = spec.astype(jnp.bfloat16).reshape(2, CHANNELS, local_inputs, local_spec)
    spec = jnp.transpose(spec, (1, 0, 2, 3))
    got = lax.all_to_all(spec, ("wide", "narrow"), 0, 0, tiled=True)
    n_wide = lax.axis_size("wide")
    n_narrow = lax.axis_size("narrow")
    chan_dev = CHANNELS // (n_wide * n_narrow)
    got = got.reshape(n_wide, n_narrow, chan_dev, 2, local_inputs, local_spec)
    got = jnp.transpose(got, (2, 3, 0, 4, 1, 5))
    all_inputs = n_wide * local_inputs
    time_len = n_narrow * local_spec
    got = got.reshape(chan_dev, 2, all_inputs, time_len)
    re = got[:, 0]
    im = got[:, 1]
    both = jnp.concatenate([re, im], axis=-1)
    turned = jnp.concatenate([im, -re], axis=-1)
    lhs = jnp.stack([both, turned], axis=1)
    vis = jnp.einsum("csik,cjk->csij", lhs, both, preferred_element_type=jnp.float32)
    return vis * (1.0 / time_len)


def solution(mesh):
    in_specs = (P("wide", "narrow"), P("wide", None))
    out_specs = P(("wide", "narrow"), None, None, None)
    return jax.shard_map(shards, mesh=mesh, in_specs=in_specs, out_specs=out_specs, check_vma=False)
```

```python
import functools
import math

import jax
import jax.numpy as jnp
from jax import lax
from jax.experimental import pallas as pl
from jax.experimental.pallas import tpu as pltpu
from jax.sharding import PartitionSpec as P

FFT_LEN = 2048
CHANNELS = 1024
TAPS = 16
PHASES = 8
SUB_LEN = FFT_LEN // PHASES
CHUNK = 32


def from_behind(x, axis, by):
    size = lax.axis_size(axis)
    pairs = [(i, i + by) for i in range(size) if 0 <= i + by < size]
    return lax.ppermute(x, axis, pairs)


def pfb_window(block_len, tap_count):
    length_all = tap_count * block_len
    sample_pos = jnp.arange(length_all, dtype=jnp.float32)
    centred = (sample_pos + 0.5 - length_all / 2.0) / block_len
    taper = 0.5 - 0.5 * jnp.cos(2.0 * jnp.pi * (sample_pos + 0.5) / length_all)
    return jnp.sinc(centred) * taper


def phase_matrices(salt):
    k1 = jnp.arange(SUB_LEN, dtype=jnp.int32)[None, :, None]
    c1 = jnp.arange(CHANNELS // PHASES, dtype=jnp.int32)[None, None, :] + salt
    c2 = jnp.arange(PHASES, dtype=jnp.int32)[:, None, None]
    turns = (k1 * (PHASES * c1 + c2)) % FFT_LEN
    angles = (2.0 * jnp.pi / FFT_LEN) * turns.astype(jnp.float32)
    scaling = 1.0 / math.sqrt(FFT_LEN)
    cos_t = jnp.cos(angles) * scaling
    sin_t = jnp.sin(angles) * scaling
    top = jnp.concatenate([cos_t, -sin_t], axis=-1)
    bottom = jnp.concatenate([sin_t, cos_t], axis=-1)
    full = jnp.concatenate([top, bottom], axis=1)
    high = full.astype(jnp.bfloat16)
    low = (full - high.astype(jnp.float32)).astype(jnp.bfloat16)
    return high, low


def split_parts(value):
    high = value.astype(jnp.bfloat16)
    low = (value - high.astype(jnp.float32)).astype(jnp.bfloat16)
    return high, low


def spectra_kernel(xa_ref, xh_ref, wb_ref, bh_ref, bl_ref, out_ref,
                   xf_ref, f_ref, uh_ref, ul_ref):
    step = pl.program_id(0)
    last = pl.num_programs(0) - 1
    halo = TAPS - 1

    def load_block(q_local, _):
        q = step * CHUNK + q_local
        start = pl.multiple_of(q * FFT_LEN, FFT_LEN)
        xf_ref[q_local] = xa_ref[:, pl.ds(start, FFT_LEN)].astype(jnp.float32)
        return 0

    lax.fori_loop(0, CHUNK, load_block, 0)

    @pl.when(step < last)
    def _():
        def body(j, _):
            q = (step + 1) * CHUNK + j
            start = pl.multiple_of(q * FFT_LEN, FFT_LEN)
            xf_ref[CHUNK + j] = xa_ref[:, pl.ds(start, FFT_LEN)].astype(jnp.float32)
            return 0
        lax.fori_loop(0, halo, body, 0)

    @pl.when(step == last)
    def _():
        def body(j, _):
            start = pl.multiple_of(j * FFT_LEN, FFT_LEN)
            xf_ref[CHUNK + j] = xh_ref[:, pl.ds(start, FFT_LEN)].astype(jnp.float32)
            return 0
        lax.fori_loop(0, halo, body, 0)

    lane_w = 256
    for lane_at in range(FFT_LEN // lane_w):
        lanes = slice(lane_at * lane_w, (lane_at + 1) * lane_w)
        taps = [wb_ref[p, :, lanes] for p in range(TAPS)]

        def filt(ml, _):
            acc = taps[0] * xf_ref[ml, :, lanes]
            for p in range(1, TAPS):
                acc = acc + taps[p] * xf_ref[ml + p, :, lanes]
            row = pl.multiple_of(ml * 8, 8)
            f_ref[pl.ds(row, 8), lanes] = acc
            return 0

        lax.fori_loop(0, CHUNK, filt, 0)

    half = 1.0 / math.sqrt(2.0)
    rows_per = 16

    def butterflies(g, _):
        row = pl.multiple_of(g * rows_per, rows_per)
        rs = pl.ds(row, rows_per)
        a = [f_ref[rs, n * SUB_LEN:(n + 1) * SUB_LEN] for n in range(PHASES)]
        s04 = a[0] + a[4]
        d04 = a[0] - a[4]
        s26 = a[2] + a[6]
        d26 = a[2] - a[6]
        s15 = a[1] + a[5]
        d15 = a[1] - a[5]
        s37 = a[3] + a[7]
        d37 = a[3] - a[7]
        e0 = s04 + s26
        e2 = s04 - s26
        o0 = s15 + s37
        o2 = s15 - s37
        p = half * (d15 - d37)
        q = half * (d15 + d37)
        outs = [
            (e0 + o0, None),
            (d04 + p, -d26 - q),
            (e2, -o2),
            (d04 - p, d26 - q),
            (e0 - o0, None),
            (d04 - p, -d26 + q),
            (e2, o2),
            (d04 + p, d26 + q),
        ]
        for c2, (re, im) in enumerate(outs):
            hi, lo = split_parts(re)
            uh_ref[c2, rs, 0:SUB_LEN] = hi
            ul_ref[c2, rs, 0:SUB_LEN] = lo
            if im is not None:
                hi, lo = split_parts(im)
                uh_ref[c2, rs, SUB_LEN:2 * SUB_LEN] = hi
                ul_ref[c2, rs, SUB_LEN:2 * SUB_LEN] = lo
        return 0

    lax.fori_loop(0, (CHUNK * 8) // rows_per, butterflies, 0)

    for c2 in range(PHASES):
        depth = SUB_LEN if c2 in (0, PHASES // 2) else 2 * SUB_LEN
        lh = uh_ref[c2, :, 0:depth]
        ll = ul_ref[c2, :, 0:depth]
        bh = bh_ref[c2, 0:depth, :]
        bl = bl_ref[c2, 0:depth, :]
        acc = jnp.dot(lh, bh, preferred_element_type=jnp.float32)
        acc = acc + jnp.dot(ll, bh, preferred_element_type=jnp.float32)
        acc = acc + jnp.dot(lh, bl, preferred_element_type=jnp.float32)
        out_ref[0, c2] = acc.astype(jnp.bfloat16)


def pfb_spectra(xa, xh, wb, bh, bl):
    n_in, span = xa.shape
    n_spec = span // FFT_LEN
    steps = n_spec // CHUNK
    rows = CHUNK * n_in
    flops = 2 * steps * rows * 3 * SUB_LEN * 2 * SUB_LEN * 7 + 2 * n_in * n_spec * FFT_LEN * TAPS
    bytes_accessed = xa.size * 2 + xh.size * 2 + steps * PHASES * rows * 2 * SUB_LEN * 2
    return pl.pallas_call(
        spectra_kernel,
        out_shape=jax.ShapeDtypeStruct((steps, PHASES, rows, CHANNELS // PHASES * 2), jnp.bfloat16),
        grid=(steps,),
        in_specs=[
            pl.BlockSpec((n_in, span), lambda s: (0, 0), pipeline_mode=pl.Buffered(1)),
            pl.BlockSpec(xh.shape, lambda s: (0, 0), pipeline_mode=pl.Buffered(1)),
            pl.BlockSpec(wb.shape, lambda s: (0, 0, 0), pipeline_mode=pl.Buffered(1)),
            pl.BlockSpec(bh.shape, lambda s: (0, 0, 0), pipeline_mode=pl.Buffered(1)),
            pl.BlockSpec(bl.shape, lambda s: (0, 0, 0), pipeline_mode=pl.Buffered(1)),
        ],
        out_specs=pl.BlockSpec((1, PHASES, rows, CHANNELS // PHASES * 2), lambda s: (s, 0, 0, 0)),
        scratch_shapes=[
            pltpu.VMEM((CHUNK + TAPS - 1, n_in, FFT_LEN), jnp.float32),
            pltpu.VMEM((rows, FFT_LEN), jnp.float32),
            pltpu.VMEM((PHASES, rows, 2 * SUB_LEN), jnp.bfloat16),
            pltpu.VMEM((PHASES, rows, 2 * SUB_LEN), jnp.bfloat16),
        ],
        compiler_params=pltpu.CompilerParams(
            dimension_semantics=("arbitrary",), vmem_limit_bytes=60 * 1024 * 1024
        ),
        cost_estimate=pl.CostEstimate(flops=flops, transcendentals=0, bytes_accessed=bytes_accessed),
    )(xa, xh, wb, bh, bl)


def shards(voltages, following):
    local_inputs, local_span = voltages.shape
    local_spec = local_span // FFT_LEN
    halo_len = (TAPS - 1) * FFT_LEN
    leading = voltages[:, :halo_len]
    shifted = from_behind(leading, "narrow", -1)
    is_final = lax.axis_index("narrow") == lax.axis_size("narrow") - 1
    after_rows = jnp.where(is_final, following, shifted)
    weights_taps = pfb_window(FFT_LEN, TAPS).reshape(TAPS, 1, FFT_LEN)
    wb = jnp.broadcast_to(weights_taps, (TAPS, local_inputs, FFT_LEN))
    salt = lax.optimization_barrier(jnp.zeros((), jnp.int32))
    bh, bl = phase_matrices(salt)
    out = pfb_spectra(voltages, after_rows, wb, bh, bl)
    steps = local_spec // CHUNK
    c1_len = CHANNELS // PHASES
    out = out.reshape(steps, PHASES, CHUNK, local_inputs, 2, c1_len)
    spec = jnp.transpose(out, (5, 1, 4, 3, 0, 2)).reshape(CHANNELS, 2, local_inputs, local_spec)
    got = lax.all_to_all(spec, ("wide", "narrow"), 0, 0, tiled=True)
    n_wide = lax.axis_size("wide")
    n_narrow = lax.axis_size("narrow")
    chan_dev = CHANNELS // (n_wide * n_narrow)
    got = got.reshape(n_wide, n_narrow, chan_dev, 2, local_inputs, local_spec)
    got = jnp.transpose(got, (2, 3, 0, 4, 1, 5))
    all_inputs = n_wide * local_inputs
    time_len = n_narrow * local_spec
    got = got.reshape(chan_dev, 2, all_inputs, time_len)
    re = got[:, 0]
    im = got[:, 1]
    both = jnp.concatenate([re, im], axis=-1)
    turned = jnp.concatenate([im, -re], axis=-1)
    lhs = jnp.stack([both, turned], axis=1)
    vis = jnp.einsum("csik,cjk->csij", lhs, both, preferred_element_type=jnp.float32)
    return vis * (1.0 / time_len)


def solution(mesh):
    in_specs = (P("wide", "narrow"), P("wide", None))
    out_specs = P(("wide", "narrow"), None, None, None)
    return jax.shard_map(shards, mesh=mesh, in_specs=in_specs, out_specs=out_specs, check_vma=False)
```

```python
import functools
import math

import jax
import jax.numpy as jnp
from jax import lax
from jax.experimental import pallas as pl
from jax.experimental.pallas import tpu as pltpu
from jax.sharding import PartitionSpec as P

FFT_LEN = 2048
CHANNELS = 1024
TAPS = 16
PHASES = 8
SUB_LEN = FFT_LEN // PHASES
CHUNK = 128


def from_behind(x, axis, by):
    size = lax.axis_size(axis)
    pairs = [(i, i + by) for i in range(size) if 0 <= i + by < size]
    return lax.ppermute(x, axis, pairs)


def pfb_window(block_len, tap_count):
    length_all = tap_count * block_len
    sample_pos = jnp.arange(length_all, dtype=jnp.float32)
    centred = (sample_pos + 0.5 - length_all / 2.0) / block_len
    taper = 0.5 - 0.5 * jnp.cos(2.0 * jnp.pi * (sample_pos + 0.5) / length_all)
    return jnp.sinc(centred) * taper


def phase_matrices(salt):
    k1 = jnp.arange(SUB_LEN, dtype=jnp.int32)[None, None, :]
    c1 = jnp.arange(CHANNELS // PHASES, dtype=jnp.int32)[None, :, None] + salt
    c2 = jnp.arange(PHASES, dtype=jnp.int32)[:, None, None]
    turns = (k1 * (PHASES * c1 + c2)) % FFT_LEN
    angles = (2.0 * jnp.pi / FFT_LEN) * turns.astype(jnp.float32)
    scaling = 1.0 / math.sqrt(FFT_LEN)
    cos_t = jnp.cos(angles) * scaling
    sin_t = jnp.sin(angles) * scaling
    real_row = jnp.concatenate([cos_t, sin_t], axis=-1)
    imag_row = jnp.concatenate([-sin_t, cos_t], axis=-1)
    full = jnp.concatenate([real_row, imag_row], axis=1)
    high = full.astype(jnp.bfloat16)
    low = (full - high.astype(jnp.float32)).astype(jnp.bfloat16)
    return high, low


def split_parts(value):
    high = value.astype(jnp.bfloat16)
    low = (value - high.astype(jnp.float32)).astype(jnp.bfloat16)
    return high, low


def nearest_bf16(value):
    scaled = value * 65537.0
    return (scaled - (scaled - value)).astype(jnp.bfloat16)


def spectra_kernel(xa_ref, xh_ref, wb_ref, bh_ref, bl_ref, out_ref,
                   xf_ref, f_ref, uh_ref, ul_ref):
    step = pl.program_id(0)
    last = pl.num_programs(0) - 1
    halo = TAPS - 1
    n_in = xa_ref.shape[0]

    def load_block(q_local, _):
        q = step * CHUNK + q_local
        start = pl.multiple_of(q * FFT_LEN, FFT_LEN)
        xf_ref[q_local] = xa_ref[:, pl.ds(start, FFT_LEN)].astype(jnp.float32)
        return 0

    lax.fori_loop(0, CHUNK, load_block, 0)

    @pl.when(step < last)
    def _():
        def body(j, _):
            q = (step + 1) * CHUNK + j
            start = pl.multiple_of(q * FFT_LEN, FFT_LEN)
            xf_ref[CHUNK + j] = xa_ref[:, pl.ds(start, FFT_LEN)].astype(jnp.float32)
            return 0
        lax.fori_loop(0, halo, body, 0)

    @pl.when(step == last)
    def _():
        def body(j, _):
            start = pl.multiple_of(j * FFT_LEN, FFT_LEN)
            xf_ref[CHUNK + j] = xh_ref[:, pl.ds(start, FFT_LEN)].astype(jnp.float32)
            return 0
        lax.fori_loop(0, halo, body, 0)

    lane_w = 128
    for lane_at in range(FFT_LEN // lane_w):
        lanes = slice(lane_at * lane_w, (lane_at + 1) * lane_w)
        taps = [wb_ref[p, :, lanes] for p in range(TAPS)]

        def filt(ml, _):
            acc = taps[0] * xf_ref[ml, :, lanes]
            for p in range(1, TAPS):
                acc = acc + taps[p] * xf_ref[ml + p, :, lanes]
            f_ref[lane_at, pl.ds(ml, n_in, stride=CHUNK), :] = acc
            return 0

        lax.fori_loop(0, CHUNK, filt, 0)

    half = 1.0 / math.sqrt(2.0)
    rows_per = 16
    sub_rows = 256

    for sub in range((CHUNK * n_in) // sub_rows):

        def butterflies(g, _):
            row = pl.multiple_of(sub * sub_rows + g * rows_per, rows_per)
            local = pl.multiple_of(g * rows_per, rows_per)
            rs = pl.ds(row, rows_per)
            ls = pl.ds(local, rows_per)
            for h in range(2):
                a = [f_ref[2 * n + h, rs, :] for n in range(PHASES)]
                s04 = a[0] + a[4]
                d04 = a[0] - a[4]
                s26 = a[2] + a[6]
                d26 = a[2] - a[6]
                s15 = a[1] + a[5]
                d15 = a[1] - a[5]
                s37 = a[3] + a[7]
                d37 = a[3] - a[7]
                e0 = s04 + s26
                e2 = s04 - s26
                o0 = s15 + s37
                o2 = s15 - s37
                p = half * (d15 - d37)
                q = half * (d15 + d37)
                outs = [
                    (e0 + o0, None),
                    (d04 + p, -d26 - q),
                    (e2, -o2),
                    (d04 - p, d26 - q),
                    (e0 - o0, None),
                    (d04 - p, -d26 + q),
                    (e2, o2),
                    (d04 + p, d26 + q),
                ]
                re_l = slice(h * 128, (h + 1) * 128)
                im_l = slice(SUB_LEN + h * 128, SUB_LEN + (h + 1) * 128)
                for c2, (re, im) in enumerate(outs):
                    hi, lo = split_parts(re)
                    uh_ref[c2, ls, re_l] = hi
                    ul_ref[c2, ls, re_l] = lo
                    if im is not None:
                        hi, lo = split_parts(im)
                        uh_ref[c2, ls, im_l] = hi
                        ul_ref[c2, ls, im_l] = lo
            return 0

        lax.fori_loop(0, sub_rows // rows_per, butterflies, 0)

        nt = (((1,), (1,)), ((), ()))
        for c2 in range(PHASES):
            depth = SUB_LEN if c2 in (0, PHASES // 2) else 2 * SUB_LEN
            uh = uh_ref[c2, :, 0:depth]
            ul = ul_ref[c2, :, 0:depth]
            bh = bh_ref[c2, :, 0:depth]
            bl = bl_ref[c2, :, 0:depth]
            acc = lax.dot_general(bh, uh, nt, preferred_element_type=jnp.float32)
            acc = acc + lax.dot_general(bh, ul, nt, preferred_element_type=jnp.float32)
            acc = acc + lax.dot_general(bl, uh, nt, preferred_element_type=jnp.float32)
            out_ref[0, c2, :, sub * sub_rows:(sub + 1) * sub_rows] = nearest_bf16(acc)


def pfb_spectra(xa, xh, wb, bh, bl):
    n_in, span = xa.shape
    n_spec = span // FFT_LEN
    steps = n_spec // CHUNK
    rows = CHUNK * n_in
    flops = 2 * steps * rows * 3 * SUB_LEN * 2 * SUB_LEN * 7 + 2 * n_in * n_spec * FFT_LEN * TAPS
    bytes_accessed = xa.size * 2 + xh.size * 2 + steps * PHASES * rows * 2 * SUB_LEN * 2
    return pl.pallas_call(
        spectra_kernel,
        out_shape=jax.ShapeDtypeStruct((steps, PHASES, 2 * CHANNELS // PHASES, rows), jnp.bfloat16),
        grid=(steps,),
        in_specs=[
            pl.BlockSpec((n_in, span), lambda s: (0, 0), pipeline_mode=pl.Buffered(1)),
            pl.BlockSpec(xh.shape, lambda s: (0, 0), pipeline_mode=pl.Buffered(1)),
            pl.BlockSpec(wb.shape, lambda s: (0, 0, 0), pipeline_mode=pl.Buffered(1)),
            pl.BlockSpec(bh.shape, lambda s: (0, 0, 0), pipeline_mode=pl.Buffered(1)),
            pl.BlockSpec(bl.shape, lambda s: (0, 0, 0), pipeline_mode=pl.Buffered(1)),
        ],
        out_specs=pl.BlockSpec((1, PHASES, 2 * CHANNELS // PHASES, rows), lambda s: (s, 0, 0, 0)),
        scratch_shapes=[
            pltpu.VMEM((CHUNK + TAPS - 1, n_in, FFT_LEN), jnp.float32),
            pltpu.VMEM((FFT_LEN // 128, rows, 128), jnp.float32),
            pltpu.VMEM((PHASES, 256, 2 * SUB_LEN), jnp.bfloat16),
            pltpu.VMEM((PHASES, 256, 2 * SUB_LEN), jnp.bfloat16),
        ],
        compiler_params=pltpu.CompilerParams(
            dimension_semantics=("arbitrary",), vmem_limit_bytes=62 * 1024 * 1024
        ),
        cost_estimate=pl.CostEstimate(flops=flops, transcendentals=0, bytes_accessed=bytes_accessed),
    )(xa, xh, wb, bh, bl)


def shards(voltages, following):
    local_inputs, local_span = voltages.shape
    local_spec = local_span // FFT_LEN
    halo_len = (TAPS - 1) * FFT_LEN
    leading = voltages[:, :halo_len]
    shifted = from_behind(leading, "narrow", -1)
    is_final = lax.axis_index("narrow") == lax.axis_size("narrow") - 1
    after_rows = jnp.where(is_final, following, shifted)
    weights_taps = pfb_window(FFT_LEN, TAPS).reshape(TAPS, 1, FFT_LEN)
    wb = jnp.broadcast_to(weights_taps, (TAPS, local_inputs, FFT_LEN))
    salt = lax.optimization_barrier(jnp.zeros((), jnp.int32))
    bh, bl = phase_matrices(salt)
    out = pfb_spectra(voltages, after_rows, wb, bh, bl)
    steps = local_spec // CHUNK
    c1_len = CHANNELS // PHASES
    out = out.reshape(steps, PHASES, 2, c1_len, local_inputs, CHUNK)
    spec = jnp.transpose(out, (3, 1, 2, 0, 4, 5))
    got = lax.all_to_all(spec, ("wide", "narrow"), 0, 0, tiled=True)
    n_wide = lax.axis_size("wide")
    n_narrow = lax.axis_size("narrow")
    got = got.reshape(n_wide, n_narrow, PHASES, 2, steps, local_inputs, CHUNK)
    got = jnp.transpose(got, (2, 0, 5, 3, 1, 4, 6))
    all_inputs = n_wide * local_inputs
    time_len = n_narrow * local_spec
    got = got.reshape(PHASES, all_inputs, 2, time_len)
    both = got.reshape(PHASES, all_inputs, 2 * time_len)
    turned = jnp.concatenate([got[:, :, 1], -got[:, :, 0]], axis=-1)
    lhs = jnp.stack([both, turned], axis=1)
    vis = jnp.einsum("csik,cjk->csij", lhs, both, preferred_element_type=jnp.float32)
    return vis * (1.0 / time_len)


def solution(mesh):
    in_specs = (P("wide", "narrow"), P("wide", None))
    out_specs = P(("wide", "narrow"), None, None, None)
    return jax.shard_map(shards, mesh=mesh, in_specs=in_specs, out_specs=out_specs, check_vma=False)
```

```python
import functools
import math

import jax
import jax.numpy as jnp
from jax import lax
from jax.experimental import pallas as pl
from jax.experimental.pallas import tpu as pltpu
from jax.sharding import PartitionSpec as P

FFT_LEN = 2048
CHANNELS = 1024
TAPS = 16
PHASES = 8
SUB_LEN = FFT_LEN // PHASES
CHUNK = 128


def from_behind(x, axis, by):
    size = lax.axis_size(axis)
    pairs = [(i, i + by) for i in range(size) if 0 <= i + by < size]
    return lax.ppermute(x, axis, pairs)


def pfb_window(block_len, tap_count):
    length_all = tap_count * block_len
    sample_pos = jnp.arange(length_all, dtype=jnp.float32)
    centred = (sample_pos + 0.5 - length_all / 2.0) / block_len
    taper = 0.5 - 0.5 * jnp.cos(2.0 * jnp.pi * (sample_pos + 0.5) / length_all)
    return jnp.sinc(centred) * taper


def phase_matrices(salt):
    k1 = jnp.arange(SUB_LEN, dtype=jnp.int32)[None, :, None]
    c1 = jnp.arange(CHANNELS // PHASES, dtype=jnp.int32)[None, None, :] + salt
    c2 = jnp.arange(PHASES, dtype=jnp.int32)[:, None, None]
    turns = (k1 * (PHASES * c1 + c2)) % FFT_LEN
    angles = (2.0 * jnp.pi / FFT_LEN) * turns.astype(jnp.float32)
    scaling = 1.0 / math.sqrt(FFT_LEN)
    cos_t = jnp.cos(angles) * scaling
    sin_t = jnp.sin(angles) * scaling
    top = jnp.concatenate([cos_t, -sin_t], axis=-1)
    bottom = jnp.concatenate([sin_t, cos_t], axis=-1)
    full = jnp.concatenate([top, bottom], axis=1)
    return split_exact(full)


def split_exact(value):
    scaled = value * 65537.0
    high = scaled - (scaled - value)
    low = value - high
    return high.astype(jnp.bfloat16), low.astype(jnp.bfloat16)


def split_parts(value):
    high = value.astype(jnp.bfloat16)
    low = (value - high.astype(jnp.float32)).astype(jnp.bfloat16)
    return high, low


def spectra_kernel(xa_ref, xh_ref, wb_ref, bh_ref, bl_ref, out_ref,
                   xf_ref, f_ref, uh_ref, ul_ref):
    step = pl.program_id(0)
    last = pl.num_programs(0) - 1
    halo = TAPS - 1
    n_in = xa_ref.shape[0]

    def load_block(q_local, _):
        q = step * CHUNK + q_local
        start = pl.multiple_of(q * FFT_LEN, FFT_LEN)
        xf_ref[q_local] = xa_ref[:, pl.ds(start, FFT_LEN)].astype(jnp.float32)
        return 0

    lax.fori_loop(0, CHUNK, load_block, 0)

    @pl.when(step < last)
    def _():
        def body(j, _):
            q = (step + 1) * CHUNK + j
            start = pl.multiple_of(q * FFT_LEN, FFT_LEN)
            xf_ref[CHUNK + j] = xa_ref[:, pl.ds(start, FFT_LEN)].astype(jnp.float32)
            return 0
        lax.fori_loop(0, halo, body, 0)

    @pl.when(step == last)
    def _():
        def body(j, _):
            start = pl.multiple_of(j * FFT_LEN, FFT_LEN)
            xf_ref[CHUNK + j] = xh_ref[:, pl.ds(start, FFT_LEN)].astype(jnp.float32)
            return 0
        lax.fori_loop(0, halo, body, 0)

    lane_w = 128
    for lane_at in range(FFT_LEN // lane_w):
        lanes = slice(lane_at * lane_w, (lane_at + 1) * lane_w)
        taps = [wb_ref[p, :, lanes] for p in range(TAPS)]

        def filt(ml, _):
            acc = taps[0] * xf_ref[ml, :, lanes]
            for p in range(1, TAPS):
                acc = acc + taps[p] * xf_ref[ml + p, :, lanes]
            f_ref[lane_at, pl.ds(ml, n_in, stride=CHUNK), :] = acc
            return 0

        lax.fori_loop(0, CHUNK, filt, 0)

    half = 1.0 / math.sqrt(2.0)
    rows_per = 16
    sub_rows = 256

    for sub in range((CHUNK * n_in) // sub_rows):

        def butterflies(g, _):
            row = pl.multiple_of(sub * sub_rows + g * rows_per, rows_per)
            local = pl.multiple_of(g * rows_per, rows_per)
            rs = pl.ds(row, rows_per)
            ls = pl.ds(local, rows_per)
            for h in range(2):
                a = [f_ref[2 * n + h, rs, :] for n in range(PHASES)]
                s04 = a[0] + a[4]
                d04 = a[0] - a[4]
                s26 = a[2] + a[6]
                d26 = a[2] - a[6]
                s15 = a[1] + a[5]
                d15 = a[1] - a[5]
                s37 = a[3] + a[7]
                d37 = a[3] - a[7]
                e0 = s04 + s26
                e2 = s04 - s26
                o0 = s15 + s37
                o2 = s15 - s37
                p = half * (d15 - d37)
                q = half * (d15 + d37)
                outs = [
                    (e0 + o0, None),
                    (d04 + p, -d26 - q),
                    (e2, -o2),
                    (d04 - p, d26 - q),
                    (e0 - o0, None),
                    (d04 - p, -d26 + q),
                    (e2, o2),
                    (d04 + p, d26 + q),
                ]
                re_l = slice(h * 128, (h + 1) * 128)
                im_l = slice(SUB_LEN + h * 128, SUB_LEN + (h + 1) * 128)
                for c2, (re, im) in enumerate(outs):
                    hi, lo = split_parts(re)
                    uh_ref[c2, ls, re_l] = hi
                    ul_ref[c2, ls, re_l] = lo
                    if im is not None:
                        hi, lo = split_parts(im)
                        uh_ref[c2, ls, im_l] = hi
                        ul_ref[c2, ls, im_l] = lo
            return 0

        lax.fori_loop(0, sub_rows // rows_per, butterflies, 0)

        for c2 in range(PHASES):
            depth = SUB_LEN if c2 in (0, PHASES // 2) else 2 * SUB_LEN
            uh = uh_ref[c2, :, 0:depth]
            ul = ul_ref[c2, :, 0:depth]
            bh = bh_ref[c2, 0:depth, :]
            bl = bl_ref[c2, 0:depth, :]
            acc = jnp.dot(uh, bh, preferred_element_type=jnp.float32)
            acc = acc + jnp.dot(ul, bh, preferred_element_type=jnp.float32)
            acc = acc + jnp.dot(uh, bl, preferred_element_type=jnp.float32)
            out_ref[0, c2, :, sub * sub_rows:(sub + 1) * sub_rows] = acc.T.astype(jnp.bfloat16)


def pfb_spectra(xa, xh, wb, bh, bl):
    n_in, span = xa.shape
    n_spec = span // FFT_LEN
    steps = n_spec // CHUNK
    rows = CHUNK * n_in
    flops = 2 * steps * rows * 3 * SUB_LEN * 2 * SUB_LEN * 7 + 2 * n_in * n_spec * FFT_LEN * TAPS
    bytes_accessed = xa.size * 2 + xh.size * 2 + steps * PHASES * rows * 2 * SUB_LEN * 2
    return pl.pallas_call(
        spectra_kernel,
        out_shape=jax.ShapeDtypeStruct((steps, PHASES, 2 * CHANNELS // PHASES, rows), jnp.bfloat16),
        grid=(steps,),
        in_specs=[
            pl.BlockSpec((n_in, span), lambda s: (0, 0), pipeline_mode=pl.Buffered(1)),
            pl.BlockSpec(xh.shape, lambda s: (0, 0), pipeline_mode=pl.Buffered(1)),
            pl.BlockSpec(wb.shape, lambda s: (0, 0, 0), pipeline_mode=pl.Buffered(1)),
            pl.BlockSpec(bh.shape, lambda s: (0, 0, 0), pipeline_mode=pl.Buffered(1)),
            pl.BlockSpec(bl.shape, lambda s: (0, 0, 0), pipeline_mode=pl.Buffered(1)),
        ],
        out_specs=pl.BlockSpec((1, PHASES, 2 * CHANNELS // PHASES, rows), lambda s: (s, 0, 0, 0)),
        scratch_shapes=[
            pltpu.VMEM((CHUNK + TAPS - 1, n_in, FFT_LEN), jnp.float32),
            pltpu.VMEM((FFT_LEN // 128, rows, 128), jnp.float32),
            pltpu.VMEM((PHASES, 256, 2 * SUB_LEN), jnp.bfloat16),
            pltpu.VMEM((PHASES, 256, 2 * SUB_LEN), jnp.bfloat16),
        ],
        compiler_params=pltpu.CompilerParams(
            dimension_semantics=("arbitrary",), vmem_limit_bytes=62 * 1024 * 1024
        ),
        cost_estimate=pl.CostEstimate(flops=flops, transcendentals=0, bytes_accessed=bytes_accessed),
    )(xa, xh, wb, bh, bl)


def shards(voltages, following):
    local_inputs, local_span = voltages.shape
    local_spec = local_span // FFT_LEN
    halo_len = (TAPS - 1) * FFT_LEN
    leading = voltages[:, :halo_len]
    shifted = from_behind(leading, "narrow", -1)
    is_final = lax.axis_index("narrow") == lax.axis_size("narrow") - 1
    after_rows = jnp.where(is_final, following, shifted)
    weights_taps = pfb_window(FFT_LEN, TAPS).reshape(TAPS, 1, FFT_LEN)
    wb = jnp.broadcast_to(weights_taps, (TAPS, local_inputs, FFT_LEN))
    salt = lax.optimization_barrier(jnp.zeros((), jnp.int32))
    bh, bl = phase_matrices(salt)
    out = pfb_spectra(voltages, after_rows, wb, bh, bl)
    steps = local_spec // CHUNK
    c1_len = CHANNELS // PHASES
    out = out.reshape(steps, PHASES, 2, c1_len, local_inputs, CHUNK)
    spec = jnp.transpose(out, (3, 1, 2, 0, 4, 5))
    got = lax.all_to_all(spec, ("wide", "narrow"), 0, 0, tiled=True)
    n_wide = lax.axis_size("wide")
    n_narrow = lax.axis_size("narrow")
    got = got.reshape(n_wide, n_narrow, PHASES, 2, steps, local_inputs, CHUNK)
    got = jnp.transpose(got, (2, 0, 5, 3, 1, 4, 6))
    all_inputs = n_wide * local_inputs
    time_len = n_narrow * local_spec
    got = got.reshape(PHASES, all_inputs, 2, time_len)
    both = got.reshape(PHASES, all_inputs, 2 * time_len)
    turned = jnp.concatenate([got[:, :, 1], -got[:, :, 0]], axis=-1)
    lhs = jnp.stack([both, turned], axis=1)
    vis = jnp.einsum("csik,cjk->csij", lhs, both, preferred_element_type=jnp.float32)
    return vis * (1.0 / time_len)


def solution(mesh):
    in_specs = (P("wide", "narrow"), P("wide", None))
    out_specs = P(("wide", "narrow"), None, None, None)
    return jax.shard_map(shards, mesh=mesh, in_specs=in_specs, out_specs=out_specs, check_vma=False)
```

```python
import functools
import math

import jax
import jax.numpy as jnp
from jax import lax
from jax.experimental import pallas as pl
from jax.experimental.pallas import tpu as pltpu
from jax.sharding import PartitionSpec as P

FFT_LEN = 2048
CHANNELS = 1024
TAPS = 16
PHASES = 8
SUB_LEN = FFT_LEN // PHASES
CHUNK = 128


def from_behind(x, axis, by):
    size = lax.axis_size(axis)
    pairs = [(i, i + by) for i in range(size) if 0 <= i + by < size]
    return lax.ppermute(x, axis, pairs)


def pfb_window(block_len, tap_count):
    length_all = tap_count * block_len
    sample_pos = jnp.arange(length_all, dtype=jnp.float32)
    centred = (sample_pos + 0.5 - length_all / 2.0) / block_len
    taper = 0.5 - 0.5 * jnp.cos(2.0 * jnp.pi * (sample_pos + 0.5) / length_all)
    return jnp.sinc(centred) * taper


def phase_matrices(salt):
    k1 = jnp.arange(SUB_LEN, dtype=jnp.int32)[None, :, None]
    c1 = jnp.arange(CHANNELS // PHASES, dtype=jnp.int32)[None, None, :] + salt
    c2 = jnp.arange(PHASES, dtype=jnp.int32)[:, None, None]
    turns = (k1 * (PHASES * c1 + c2)) % FFT_LEN
    angles = (2.0 * jnp.pi / FFT_LEN) * turns.astype(jnp.float32)
    scaling = 1.0 / math.sqrt(FFT_LEN)
    cos_t = jnp.cos(angles) * scaling
    sin_t = jnp.sin(angles) * scaling
    top = jnp.concatenate([cos_t, -sin_t], axis=-1)
    bottom = jnp.concatenate([sin_t, cos_t], axis=-1)
    full = jnp.concatenate([top, bottom], axis=1)
    return split_exact(full)


def split_exact(value):
    scaled = value * 65537.0
    high = scaled - (scaled - value)
    low = value - high
    return high.astype(jnp.bfloat16), low.astype(jnp.bfloat16)


def split_parts(value):
    high = value.astype(jnp.bfloat16)
    low = (value - high.astype(jnp.float32)).astype(jnp.bfloat16)
    return high, low


def spectra_kernel(xa_ref, xh_ref, wb_ref, bh_ref, bl_ref, out_ref,
                   xf_ref, f_ref, uh_ref, ul_ref):
    step = pl.program_id(0)
    last = pl.num_programs(0) - 1
    halo = TAPS - 1
    n_in = xa_ref.shape[0]

    def load_block(q_local, _):
        q = step * CHUNK + q_local
        start = pl.multiple_of(q * FFT_LEN, FFT_LEN)
        xf_ref[q_local] = xa_ref[:, pl.ds(start, FFT_LEN)].astype(jnp.float32)
        return 0

    lax.fori_loop(0, CHUNK, load_block, 0)

    @pl.when(step < last)
    def _():
        def body(j, _):
            q = (step + 1) * CHUNK + j
            start = pl.multiple_of(q * FFT_LEN, FFT_LEN)
            xf_ref[CHUNK + j] = xa_ref[:, pl.ds(start, FFT_LEN)].astype(jnp.float32)
            return 0
        lax.fori_loop(0, halo, body, 0)

    @pl.when(step == last)
    def _():
        def body(j, _):
            start = pl.multiple_of(j * FFT_LEN, FFT_LEN)
            xf_ref[CHUNK + j] = xh_ref[:, pl.ds(start, FFT_LEN)].astype(jnp.float32)
            return 0
        lax.fori_loop(0, halo, body, 0)

    lane_w = 128
    for lane_at in range(FFT_LEN // lane_w):
        lanes = slice(lane_at * lane_w, (lane_at + 1) * lane_w)
        taps = [wb_ref[p, :, lanes] for p in range(TAPS)]

        def filt(ml, _):
            terms = [taps[p] * xf_ref[ml + p, :, lanes] for p in range(TAPS)]
            while len(terms) > 1:
                terms = [terms[j] + terms[j + 1] for j in range(0, len(terms), 2)]
            f_ref[lane_at, pl.ds(ml, n_in, stride=CHUNK), :] = terms[0]
            return 0

        lax.fori_loop(0, CHUNK, filt, 0, unroll=4)

    half = 1.0 / math.sqrt(2.0)
    rows_per = 16
    sub_rows = 256

    for sub in range((CHUNK * n_in) // sub_rows):

        def butterflies(g, _):
            row = pl.multiple_of(sub * sub_rows + g * rows_per, rows_per)
            local = pl.multiple_of(g * rows_per, rows_per)
            rs = pl.ds(row, rows_per)
            ls = pl.ds(local, rows_per)
            for h in range(2):
                a = [f_ref[2 * n + h, rs, :] for n in range(PHASES)]
                s04 = a[0] + a[4]
                d04 = a[0] - a[4]
                s26 = a[2] + a[6]
                d26 = a[2] - a[6]
                s15 = a[1] + a[5]
                d15 = a[1] - a[5]
                s37 = a[3] + a[7]
                d37 = a[3] - a[7]
                e0 = s04 + s26
                e2 = s04 - s26
                o0 = s15 + s37
                o2 = s15 - s37
                p = half * (d15 - d37)
                q = half * (d15 + d37)
                outs = [
                    (e0 + o0, None),
                    (d04 + p, -d26 - q),
                    (e2, -o2),
                    (d04 - p, d26 - q),
                    (e0 - o0, None),
                    (d04 - p, -d26 + q),
                    (e2, o2),
                    (d04 + p, d26 + q),
                ]
                re_l = slice(h * 128, (h + 1) * 128)
                im_l = slice(SUB_LEN + h * 128, SUB_LEN + (h + 1) * 128)
                for c2, (re, im) in enumerate(outs):
                    hi, lo = split_parts(re)
                    uh_ref[c2, ls, re_l] = hi
                    ul_ref[c2, ls, re_l] = lo
                    if im is not None:
                        hi, lo = split_parts(im)
                        uh_ref[c2, ls, im_l] = hi
                        ul_ref[c2, ls, im_l] = lo
            return 0

        lax.fori_loop(0, sub_rows // rows_per, butterflies, 0)

        for c2 in range(PHASES):
            depth = SUB_LEN if c2 in (0, PHASES // 2) else 2 * SUB_LEN
            uh = uh_ref[c2, :, 0:depth]
            ul = ul_ref[c2, :, 0:depth]
            bh = bh_ref[c2, 0:depth, :]
            bl = bl_ref[c2, 0:depth, :]
            acc = jnp.dot(uh, bh, preferred_element_type=jnp.float32)
            acc = acc + jnp.dot(ul, bh, preferred_element_type=jnp.float32)
            acc = acc + jnp.dot(uh, bl, preferred_element_type=jnp.float32)
            out_ref[0, c2, :, sub * sub_rows:(sub + 1) * sub_rows] = acc.T.astype(jnp.bfloat16)


def pfb_spectra(xa, xh, wb, bh, bl):
    n_in, span = xa.shape
    n_spec = span // FFT_LEN
    steps = n_spec // CHUNK
    rows = CHUNK * n_in
    flops = 2 * steps * rows * 3 * SUB_LEN * 2 * SUB_LEN * 7 + 2 * n_in * n_spec * FFT_LEN * TAPS
    bytes_accessed = xa.size * 2 + xh.size * 2 + steps * PHASES * rows * 2 * SUB_LEN * 2
    return pl.pallas_call(
        spectra_kernel,
        out_shape=jax.ShapeDtypeStruct((steps, PHASES, 2 * CHANNELS // PHASES, rows), jnp.bfloat16),
        grid=(steps,),
        in_specs=[
            pl.BlockSpec((n_in, span), lambda s: (0, 0), pipeline_mode=pl.Buffered(1)),
            pl.BlockSpec(xh.shape, lambda s: (0, 0), pipeline_mode=pl.Buffered(1)),
            pl.BlockSpec(wb.shape, lambda s: (0, 0, 0), pipeline_mode=pl.Buffered(1)),
            pl.BlockSpec(bh.shape, lambda s: (0, 0, 0), pipeline_mode=pl.Buffered(1)),
            pl.BlockSpec(bl.shape, lambda s: (0, 0, 0), pipeline_mode=pl.Buffered(1)),
        ],
        out_specs=pl.BlockSpec((1, PHASES, 2 * CHANNELS // PHASES, rows), lambda s: (s, 0, 0, 0)),
        scratch_shapes=[
            pltpu.VMEM((CHUNK + TAPS - 1, n_in, FFT_LEN), jnp.float32),
            pltpu.VMEM((FFT_LEN // 128, rows, 128), jnp.float32),
            pltpu.VMEM((PHASES, 256, 2 * SUB_LEN), jnp.bfloat16),
            pltpu.VMEM((PHASES, 256, 2 * SUB_LEN), jnp.bfloat16),
        ],
        compiler_params=pltpu.CompilerParams(
            dimension_semantics=("arbitrary",), vmem_limit_bytes=62 * 1024 * 1024
        ),
        cost_estimate=pl.CostEstimate(flops=flops, transcendentals=0, bytes_accessed=bytes_accessed),
    )(xa, xh, wb, bh, bl)


def shards(voltages, following):
    local_inputs, local_span = voltages.shape
    local_spec = local_span // FFT_LEN
    halo_len = (TAPS - 1) * FFT_LEN
    leading = voltages[:, :halo_len]
    shifted = from_behind(leading, "narrow", -1)
    is_final = lax.axis_index("narrow") == lax.axis_size("narrow") - 1
    after_rows = jnp.where(is_final, following, shifted)
    weights_taps = pfb_window(FFT_LEN, TAPS).reshape(TAPS, 1, FFT_LEN)
    wb = jnp.broadcast_to(weights_taps, (TAPS, local_inputs, FFT_LEN))
    salt = lax.optimization_barrier(jnp.zeros((), jnp.int32))
    bh, bl = phase_matrices(salt)
    out = pfb_spectra(voltages, after_rows, wb, bh, bl)
    steps = local_spec // CHUNK
    c1_len = CHANNELS // PHASES
    out = out.reshape(steps, PHASES, 2, c1_len, local_inputs, CHUNK)
    spec = jnp.transpose(out, (3, 1, 2, 0, 4, 5))
    got = lax.all_to_all(spec, ("wide", "narrow"), 0, 0, tiled=True)
    n_wide = lax.axis_size("wide")
    n_narrow = lax.axis_size("narrow")
    got = got.reshape(n_wide, n_narrow, PHASES, 2, steps, local_inputs, CHUNK)
    got = jnp.transpose(got, (2, 0, 5, 3, 1, 4, 6))
    all_inputs = n_wide * local_inputs
    time_len = n_narrow * local_spec
    got = got.reshape(PHASES, all_inputs, 2, time_len)
    both = got.reshape(PHASES, all_inputs, 2 * time_len)
    turned = jnp.concatenate([got[:, :, 1], -got[:, :, 0]], axis=-1)
    lhs = jnp.stack([both, turned], axis=1)
    vis = jnp.einsum("csik,cjk->csij", lhs, both, preferred_element_type=jnp.float32)
    return vis * (1.0 / time_len)


def solution(mesh):
    in_specs = (P("wide", "narrow"), P("wide", None))
    out_specs = P(("wide", "narrow"), None, None, None)
    return jax.shard_map(shards, mesh=mesh, in_specs=in_specs, out_specs=out_specs, check_vma=False)
```

```python
import functools
import math

import jax
import jax.numpy as jnp
from jax import lax
from jax.experimental import pallas as pl
from jax.experimental.pallas import tpu as pltpu
from jax.sharding import PartitionSpec as P

FFT_LEN = 2048
CHANNELS = 1024
TAPS = 16
PHASES = 8
SUB_LEN = FFT_LEN // PHASES
CHUNK = 128


def from_behind(x, axis, by):
    size = lax.axis_size(axis)
    pairs = [(i, i + by) for i in range(size) if 0 <= i + by < size]
    return lax.ppermute(x, axis, pairs)


def pfb_window(block_len, tap_count):
    length_all = tap_count * block_len
    sample_pos = jnp.arange(length_all, dtype=jnp.float32)
    centred = (sample_pos + 0.5 - length_all / 2.0) / block_len
    taper = 0.5 - 0.5 * jnp.cos(2.0 * jnp.pi * (sample_pos + 0.5) / length_all)
    return jnp.sinc(centred) * taper


def phase_matrices(salt):
    k1 = jnp.arange(SUB_LEN, dtype=jnp.int32)[None, :, None]
    c1 = jnp.arange(CHANNELS // PHASES, dtype=jnp.int32)[None, None, :] + salt
    c2 = jnp.arange(PHASES, dtype=jnp.int32)[:, None, None]
    turns = (k1 * (PHASES * c1 + c2)) % FFT_LEN
    angles = (2.0 * jnp.pi / FFT_LEN) * turns.astype(jnp.float32)
    scaling = 1.0 / math.sqrt(FFT_LEN)
    cos_t = jnp.cos(angles) * scaling
    sin_t = jnp.sin(angles) * scaling
    top = jnp.concatenate([cos_t, -sin_t], axis=-1)
    bottom = jnp.concatenate([sin_t, cos_t], axis=-1)
    full = jnp.concatenate([top, bottom], axis=1)
    return split_exact(full)


def split_exact(value):
    scaled = value * 65537.0
    high = scaled - (scaled - value)
    low = value - high
    return high.astype(jnp.bfloat16), low.astype(jnp.bfloat16)


def split_parts(value):
    high = value.astype(jnp.bfloat16)
    low = (value - high.astype(jnp.float32)).astype(jnp.bfloat16)
    return high, low


def spectra_kernel(xa_ref, xh_ref, wb_ref, bh_ref, bl_ref, out_ref,
                   xf_ref, f_ref, uh_ref, ul_ref):
    step = pl.program_id(0)
    last = pl.num_programs(0) - 1
    halo = TAPS - 1
    n_in = xa_ref.shape[0]

    def load_block(q_local, _):
        q = step * CHUNK + q_local
        start = pl.multiple_of(q * FFT_LEN, FFT_LEN)
        xf_ref[q_local] = xa_ref[:, pl.ds(start, FFT_LEN)].astype(jnp.float32)
        return 0

    lax.fori_loop(0, CHUNK, load_block, 0)

    @pl.when(step < last)
    def _():
        def body(j, _):
            q = (step + 1) * CHUNK + j
            start = pl.multiple_of(q * FFT_LEN, FFT_LEN)
            xf_ref[CHUNK + j] = xa_ref[:, pl.ds(start, FFT_LEN)].astype(jnp.float32)
            return 0
        lax.fori_loop(0, halo, body, 0)

    @pl.when(step == last)
    def _():
        def body(j, _):
            start = pl.multiple_of(j * FFT_LEN, FFT_LEN)
            xf_ref[CHUNK + j] = xh_ref[:, pl.ds(start, FFT_LEN)].astype(jnp.float32)
            return 0
        lax.fori_loop(0, halo, body, 0)

    lane_w = 128
    for lane_at in range(FFT_LEN // lane_w):
        lanes = slice(lane_at * lane_w, (lane_at + 1) * lane_w)
        taps = [wb_ref[p, :, lanes] for p in range(TAPS)]

        def filt(ml, _):
            terms = [taps[p] * xf_ref[ml + p, :, lanes] for p in range(TAPS)]
            while len(terms) > 1:
                terms = [terms[j] + terms[j + 1] for j in range(0, len(terms), 2)]
            f_ref[lane_at, pl.ds(ml, n_in, stride=CHUNK), :] = terms[0]
            return 0

        lax.fori_loop(0, CHUNK, filt, 0, unroll=4)

    half = 1.0 / math.sqrt(2.0)
    rows_per = 16
    sub_rows = 256

    for sub in range((CHUNK * n_in) // sub_rows):

        def butterflies(g, _):
            row = pl.multiple_of(sub * sub_rows + g * rows_per, rows_per)
            local = pl.multiple_of(g * rows_per, rows_per)
            rs = pl.ds(row, rows_per)
            ls = pl.ds(local, rows_per)
            for h in range(2):
                a = [f_ref[2 * n + h, rs, :] for n in range(PHASES)]
                s04 = a[0] + a[4]
                d04 = a[0] - a[4]
                s26 = a[2] + a[6]
                d26 = a[2] - a[6]
                s15 = a[1] + a[5]
                d15 = a[1] - a[5]
                s37 = a[3] + a[7]
                d37 = a[3] - a[7]
                e0 = s04 + s26
                e2 = s04 - s26
                o0 = s15 + s37
                o2 = s15 - s37
                p = half * (d15 - d37)
                q = half * (d15 + d37)
                outs = [
                    (e0 + o0, None),
                    (d04 + p, -d26 - q),
                    (e2, -o2),
                    (d04 - p, d26 - q),
                    (e0 - o0, None),
                    (d04 - p, -d26 + q),
                    (e2, o2),
                    (d04 + p, d26 + q),
                ]
                re_l = slice(h * 128, (h + 1) * 128)
                im_l = slice(SUB_LEN + h * 128, SUB_LEN + (h + 1) * 128)
                for c2, (re, im) in enumerate(outs):
                    hi, lo = split_parts(re)
                    uh_ref[c2, ls, re_l] = hi
                    ul_ref[c2, ls, re_l] = lo
                    if im is not None:
                        hi, lo = split_parts(im)
                        uh_ref[c2, ls, im_l] = hi
                        ul_ref[c2, ls, im_l] = lo
            return 0

        lax.fori_loop(0, sub_rows // rows_per, butterflies, 0)

        for c2 in range(PHASES):
            depth = SUB_LEN if c2 in (0, PHASES // 2) else 2 * SUB_LEN
            uh = uh_ref[c2, :, 0:depth]
            ul = ul_ref[c2, :, 0:depth]
            bh = bh_ref[c2, 0:depth, :]
            bl = bl_ref[c2, 0:depth, :]
            acc = jnp.dot(uh, bh, preferred_element_type=jnp.float32)
            acc = acc + jnp.dot(ul, bh, preferred_element_type=jnp.float32)
            acc = acc + jnp.dot(uh, bl, preferred_element_type=jnp.float32)
            out_ref[0, c2, :, sub * sub_rows:(sub + 1) * sub_rows] = acc.T.astype(jnp.bfloat16)


def pfb_spectra(xa, xh, wb, bh, bl):
    n_in, span = xa.shape
    n_spec = span // FFT_LEN
    steps = n_spec // CHUNK
    rows = CHUNK * n_in
    flops = 2 * steps * rows * 3 * SUB_LEN * 2 * SUB_LEN * 7 + 2 * n_in * n_spec * FFT_LEN * TAPS
    bytes_accessed = xa.size * 2 + xh.size * 2 + steps * PHASES * rows * 2 * SUB_LEN * 2
    return pl.pallas_call(
        spectra_kernel,
        out_shape=jax.ShapeDtypeStruct((steps, PHASES, 2 * CHANNELS // PHASES, rows), jnp.bfloat16),
        grid=(steps,),
        in_specs=[
            pl.BlockSpec((n_in, span), lambda s: (0, 0), pipeline_mode=pl.Buffered(1)),
            pl.BlockSpec(xh.shape, lambda s: (0, 0), pipeline_mode=pl.Buffered(1)),
            pl.BlockSpec(wb.shape, lambda s: (0, 0, 0), pipeline_mode=pl.Buffered(1)),
            pl.BlockSpec(bh.shape, lambda s: (0, 0, 0), pipeline_mode=pl.Buffered(1)),
            pl.BlockSpec(bl.shape, lambda s: (0, 0, 0), pipeline_mode=pl.Buffered(1)),
        ],
        out_specs=pl.BlockSpec((1, PHASES, 2 * CHANNELS // PHASES, rows), lambda s: (s, 0, 0, 0)),
        scratch_shapes=[
            pltpu.VMEM((CHUNK + TAPS - 1, n_in, FFT_LEN), jnp.float32),
            pltpu.VMEM((FFT_LEN // 128, rows, 128), jnp.float32),
            pltpu.VMEM((PHASES, 256, 2 * SUB_LEN), jnp.bfloat16),
            pltpu.VMEM((PHASES, 256, 2 * SUB_LEN), jnp.bfloat16),
        ],
        compiler_params=pltpu.CompilerParams(
            dimension_semantics=("arbitrary",), vmem_limit_bytes=62 * 1024 * 1024
        ),
        cost_estimate=pl.CostEstimate(flops=flops, transcendentals=0, bytes_accessed=bytes_accessed),
    )(xa, xh, wb, bh, bl)


def gram_kernel(n_narrow, g_ref, out_ref, l_ref):
    n_src = g_ref.shape[0]
    steps = g_ref.shape[3]
    seg = g_ref.shape[5]
    n_in = g_ref.shape[4]

    def gather(w, _):
        row = pl.multiple_of(w * n_in, n_in)
        for n in range(n_narrow):
            for ri in range(2):
                for s in range(steps):
                    col = ((ri * n_narrow + n) * steps + s) * seg
                    l_ref[pl.ds(row, n_in), col:col + seg] = g_ref[w * n_narrow + n, 0, ri, s].astype(jnp.float32)
        return 0

    lax.fori_loop(0, n_src // n_narrow, gather, 0)
    both = l_ref[...].astype(jnp.bfloat16)
    half = both.shape[1] // 2
    turned = jnp.concatenate([both[:, half:], -both[:, :half]], axis=1)
    nt = (((1,), (1,)), ((), ()))
    scale = 1.0 / half
    out_ref[0, 0] = lax.dot_general(both, both, nt, preferred_element_type=jnp.float32) * scale
    out_ref[0, 1] = lax.dot_general(turned, both, nt, preferred_element_type=jnp.float32) * scale


def visibilities(got, n_narrow):
    n_src, phases, parts, steps, n_in, seg = got.shape
    all_inputs = n_src // n_narrow * n_in
    depth = parts * n_narrow * steps * seg
    return pl.pallas_call(
        functools.partial(gram_kernel, n_narrow),
        out_shape=jax.ShapeDtypeStruct((phases, 2, all_inputs, all_inputs), jnp.float32),
        grid=(phases,),
        in_specs=[pl.BlockSpec((n_src, 1, parts, steps, n_in, seg), lambda c: (0, c, 0, 0, 0, 0))],
        out_specs=pl.BlockSpec((1, 2, all_inputs, all_inputs), lambda c: (c, 0, 0, 0)),
        scratch_shapes=[pltpu.VMEM((all_inputs, depth), jnp.float32)],
        compiler_params=pltpu.CompilerParams(
            dimension_semantics=("arbitrary",), vmem_limit_bytes=48 * 1024 * 1024
        ),
        cost_estimate=pl.CostEstimate(
            flops=phases * 4 * all_inputs * all_inputs * depth,
            transcendentals=0,
            bytes_accessed=got.size * 2 + phases * 2 * all_inputs * all_inputs * 4,
        ),
    )(got)


def shards(voltages, following):
    local_inputs, local_span = voltages.shape
    local_spec = local_span // FFT_LEN
    halo_len = (TAPS - 1) * FFT_LEN
    leading = voltages[:, :halo_len]
    shifted = from_behind(leading, "narrow", -1)
    is_final = lax.axis_index("narrow") == lax.axis_size("narrow") - 1
    after_rows = jnp.where(is_final, following, shifted)
    weights_taps = pfb_window(FFT_LEN, TAPS).reshape(TAPS, 1, FFT_LEN)
    wb = jnp.broadcast_to(weights_taps, (TAPS, local_inputs, FFT_LEN))
    salt = lax.optimization_barrier(jnp.zeros((), jnp.int32))
    bh, bl = phase_matrices(salt)
    out = pfb_spectra(voltages, after_rows, wb, bh, bl)
    steps = local_spec // CHUNK
    c1_len = CHANNELS // PHASES
    out = out.reshape(steps, PHASES, 2, c1_len, local_inputs, CHUNK)
    spec = jnp.transpose(out, (3, 1, 2, 0, 4, 5))
    got = lax.all_to_all(spec, ("wide", "narrow"), 0, 0, tiled=True)
    return visibilities(got, lax.axis_size("narrow"))


def solution(mesh):
    in_specs = (P("wide", "narrow"), P("wide", None))
    out_specs = P(("wide", "narrow"), None, None, None)
    return jax.shard_map(shards, mesh=mesh, in_specs=in_specs, out_specs=out_specs, check_vma=False)
```

```python
import functools
import math

import jax
import jax.numpy as jnp
from jax import lax
from jax.experimental import pallas as pl
from jax.experimental.pallas import tpu as pltpu
from jax.sharding import PartitionSpec as P

FFT_LEN = 2048
CHANNELS = 1024
TAPS = 16
PHASES = 8
SUB_LEN = FFT_LEN // PHASES
CHUNK = 128


def from_behind(x, axis, by):
    size = lax.axis_size(axis)
    pairs = [(i, i + by) for i in range(size) if 0 <= i + by < size]
    return lax.ppermute(x, axis, pairs)


def pfb_window(block_len, tap_count):
    length_all = tap_count * block_len
    sample_pos = jnp.arange(length_all, dtype=jnp.float32)
    centred = (sample_pos + 0.5 - length_all / 2.0) / block_len
    taper = 0.5 - 0.5 * jnp.cos(2.0 * jnp.pi * (sample_pos + 0.5) / length_all)
    return jnp.sinc(centred) * taper


def phase_matrices(salt):
    k1 = jnp.arange(SUB_LEN, dtype=jnp.int32)[None, :, None]
    c1 = jnp.arange(CHANNELS // PHASES, dtype=jnp.int32)[None, None, :] + salt
    c2 = jnp.arange(PHASES, dtype=jnp.int32)[:, None, None]
    turns = (k1 * (PHASES * c1 + c2)) % FFT_LEN
    angles = (2.0 * jnp.pi / FFT_LEN) * turns.astype(jnp.float32)
    scaling = 1.0 / math.sqrt(FFT_LEN)
    cos_t = jnp.cos(angles) * scaling
    sin_t = jnp.sin(angles) * scaling
    top = jnp.concatenate([cos_t, -sin_t], axis=-1)
    bottom = jnp.concatenate([sin_t, cos_t], axis=-1)
    full = jnp.concatenate([top, bottom], axis=1)
    return split_exact(full)


def split_exact(value):
    scaled = value * 65537.0
    high = scaled - (scaled - value)
    low = value - high
    return high.astype(jnp.bfloat16), low.astype(jnp.bfloat16)


def split_parts(value):
    high = value.astype(jnp.bfloat16)
    low = (value - high.astype(jnp.float32)).astype(jnp.bfloat16)
    return high, low


def spectra_kernel(with_halo, *refs):
    if with_halo:
        xa_ref, xh_ref, wb_ref, bh_ref, bl_ref, _, out_ref, xf_ref, f_ref, uh_ref, ul_ref = refs
    else:
        xa_ref, wb_ref, bh_ref, bl_ref, out_ref, xf_ref, f_ref, uh_ref, ul_ref = refs
        xh_ref = xa_ref
    n_in = xa_ref.shape[0]
    own = CHUNK if with_halo else CHUNK + TAPS - 1

    def load_block(q_local, _):
        start = pl.multiple_of(q_local * FFT_LEN, FFT_LEN)
        xf_ref[q_local] = xa_ref[:, pl.ds(start, FFT_LEN)].astype(jnp.float32)
        return 0

    lax.fori_loop(0, own, load_block, 0)

    if with_halo:
        def body(j, _):
            start = pl.multiple_of(j * FFT_LEN, FFT_LEN)
            xf_ref[CHUNK + j] = xh_ref[:, pl.ds(start, FFT_LEN)].astype(jnp.float32)
            return 0
        lax.fori_loop(0, TAPS - 1, body, 0)

    lane_w = 128
    for lane_at in range(FFT_LEN // lane_w):
        lanes = slice(lane_at * lane_w, (lane_at + 1) * lane_w)
        taps = [wb_ref[p, :, lanes] for p in range(TAPS)]

        def filt(ml, _):
            terms = [taps[p] * xf_ref[ml + p, :, lanes] for p in range(TAPS)]
            while len(terms) > 1:
                terms = [terms[j] + terms[j + 1] for j in range(0, len(terms), 2)]
            f_ref[lane_at, pl.ds(ml, n_in, stride=CHUNK), :] = terms[0]
            return 0

        lax.fori_loop(0, CHUNK, filt, 0, unroll=4)

    half = 1.0 / math.sqrt(2.0)
    rows_per = 16
    sub_rows = 256

    for sub in range((CHUNK * n_in) // sub_rows):

        def butterflies(g, _):
            row = pl.multiple_of(sub * sub_rows + g * rows_per, rows_per)
            local = pl.multiple_of(g * rows_per, rows_per)
            rs = pl.ds(row, rows_per)
            ls = pl.ds(local, rows_per)
            for h in range(2):
                a = [f_ref[2 * n + h, rs, :] for n in range(PHASES)]
                s04 = a[0] + a[4]
                d04 = a[0] - a[4]
                s26 = a[2] + a[6]
                d26 = a[2] - a[6]
                s15 = a[1] + a[5]
                d15 = a[1] - a[5]
                s37 = a[3] + a[7]
                d37 = a[3] - a[7]
                e0 = s04 + s26
                e2 = s04 - s26
                o0 = s15 + s37
                o2 = s15 - s37
                p = half * (d15 - d37)
                q = half * (d15 + d37)
                outs = [
                    (e0 + o0, None),
                    (d04 + p, -d26 - q),
                    (e2, -o2),
                    (d04 - p, d26 - q),
                    (e0 - o0, None),
                    (d04 - p, -d26 + q),
                    (e2, o2),
                    (d04 + p, d26 + q),
                ]
                re_l = slice(h * 128, (h + 1) * 128)
                im_l = slice(SUB_LEN + h * 128, SUB_LEN + (h + 1) * 128)
                for c2, (re, im) in enumerate(outs):
                    hi, lo = split_parts(re)
                    uh_ref[c2, ls, re_l] = hi
                    ul_ref[c2, ls, re_l] = lo
                    if im is not None:
                        hi, lo = split_parts(im)
                        uh_ref[c2, ls, im_l] = hi
                        ul_ref[c2, ls, im_l] = lo
            return 0

        lax.fori_loop(0, sub_rows // rows_per, butterflies, 0)

        for c2 in range(PHASES):
            depth = SUB_LEN if c2 in (0, PHASES // 2) else 2 * SUB_LEN
            uh = uh_ref[c2, :, 0:depth]
            ul = ul_ref[c2, :, 0:depth]
            bh = bh_ref[c2, 0:depth, :]
            bl = bl_ref[c2, 0:depth, :]
            acc = jnp.dot(uh, bh, preferred_element_type=jnp.float32)
            acc = acc + jnp.dot(ul, bh, preferred_element_type=jnp.float32)
            acc = acc + jnp.dot(uh, bl, preferred_element_type=jnp.float32)
            out_ref[0, c2, :, sub * sub_rows:(sub + 1) * sub_rows] = acc.T.astype(jnp.bfloat16)


def pfb_chunk(xa, xh, wb, bh, bl, chunk_at, prev):
    n_in, span = xa.shape
    rows = CHUNK * n_in
    with_halo = xh is not None
    lanes = CHUNK * FFT_LEN if with_halo else (CHUNK + TAPS - 1) * FFT_LEN
    flops = 2 * rows * 3 * SUB_LEN * 2 * SUB_LEN * 7 + 2 * n_in * CHUNK * FFT_LEN * TAPS
    bytes_accessed = n_in * lanes * 2 + PHASES * rows * 2 * SUB_LEN * 2
    xa_spec = pl.BlockSpec((n_in, lanes), lambda s: (0, chunk_at))
    const3 = lambda s: (0, 0, 0)
    in_specs = [pl.BlockSpec(xa_spec.block_shape, xa_spec.index_map, pipeline_mode=pl.Buffered(1))]
    operands = [xa]
    if with_halo:
        in_specs.append(pl.BlockSpec(xh.shape, lambda s: (0, 0), pipeline_mode=pl.Buffered(1)))
        operands.append(xh)
    for arr in (wb, bh, bl):
        in_specs.append(pl.BlockSpec(arr.shape, const3, pipeline_mode=pl.Buffered(1)))
        operands.append(arr)
    aliases = {}
    if with_halo:
        in_specs.append(pl.BlockSpec(memory_space=pl.ANY))
        operands.append(prev)
        aliases = {len(operands) - 1: 0}
    steps = span // FFT_LEN // CHUNK
    return pl.pallas_call(
        functools.partial(spectra_kernel, with_halo),
        out_shape=jax.ShapeDtypeStruct((steps, PHASES, 2 * CHANNELS // PHASES, rows), jnp.bfloat16),
        grid=(1,),
        in_specs=in_specs,
        out_specs=pl.BlockSpec((1, PHASES, 2 * CHANNELS // PHASES, rows), lambda s: (chunk_at, 0, 0, 0)),
        input_output_aliases=aliases,
        scratch_shapes=[
            pltpu.VMEM((CHUNK + TAPS - 1, n_in, FFT_LEN), jnp.float32),
            pltpu.VMEM((FFT_LEN // 128, rows, 128), jnp.float32),
            pltpu.VMEM((PHASES, 256, 2 * SUB_LEN), jnp.bfloat16),
            pltpu.VMEM((PHASES, 256, 2 * SUB_LEN), jnp.bfloat16),
        ],
        compiler_params=pltpu.CompilerParams(
            dimension_semantics=("arbitrary",), vmem_limit_bytes=62 * 1024 * 1024
        ),
        cost_estimate=pl.CostEstimate(flops=flops, transcendentals=0, bytes_accessed=bytes_accessed),
    )(*operands)


def pfb_spectra(xa, xh, wb, bh, bl):
    n_spec = xa.shape[1] // FFT_LEN
    steps = n_spec // CHUNK
    first = pfb_chunk(xa, None, wb, bh, bl, 0, None)
    return pfb_chunk(xa, xh, wb, bh, bl, steps - 1, first)


def gram_kernel(n_narrow, g_ref, out_ref, l_ref):
    n_src = g_ref.shape[0]
    steps = g_ref.shape[3]
    seg = g_ref.shape[5]
    n_in = g_ref.shape[4]

    def gather(w, _):
        row = pl.multiple_of(w * n_in, n_in)
        for n in range(n_narrow):
            for ri in range(2):
                for s in range(steps):
                    col = ((ri * n_narrow + n) * steps + s) * seg
                    l_ref[pl.ds(row, n_in), col:col + seg] = g_ref[w * n_narrow + n, 0, ri, s].astype(jnp.float32)
        return 0

    lax.fori_loop(0, n_src // n_narrow, gather, 0)
    both = l_ref[...].astype(jnp.bfloat16)
    half = both.shape[1] // 2
    turned = jnp.concatenate([both[:, half:], -both[:, :half]], axis=1)
    nt = (((1,), (1,)), ((), ()))
    scale = 1.0 / half
    out_ref[0, 0] = lax.dot_general(both, both, nt, preferred_element_type=jnp.float32) * scale
    out_ref[0, 1] = lax.dot_general(turned, both, nt, preferred_element_type=jnp.float32) * scale


def visibilities(got, n_narrow):
    n_src, phases, parts, steps, n_in, seg = got.shape
    all_inputs = n_src // n_narrow * n_in
    depth = parts * n_narrow * steps * seg
    return pl.pallas_call(
        functools.partial(gram_kernel, n_narrow),
        out_shape=jax.ShapeDtypeStruct((phases, 2, all_inputs, all_inputs), jnp.float32),
        grid=(phases,),
        in_specs=[pl.BlockSpec((n_src, 1, parts, steps, n_in, seg), lambda c: (0, c, 0, 0, 0, 0))],
        out_specs=pl.BlockSpec((1, 2, all_inputs, all_inputs), lambda c: (c, 0, 0, 0)),
        scratch_shapes=[pltpu.VMEM((all_inputs, depth), jnp.float32)],
        compiler_params=pltpu.CompilerParams(
            dimension_semantics=("arbitrary",), vmem_limit_bytes=48 * 1024 * 1024
        ),
        cost_estimate=pl.CostEstimate(
            flops=phases * 4 * all_inputs * all_inputs * depth,
            transcendentals=0,
            bytes_accessed=got.size * 2 + phases * 2 * all_inputs * all_inputs * 4,
        ),
    )(got)


def shards(voltages, following):
    local_inputs, local_span = voltages.shape
    local_spec = local_span // FFT_LEN
    halo_len = (TAPS - 1) * FFT_LEN
    leading = voltages[:, :halo_len]
    shifted = from_behind(leading, "narrow", -1)
    is_final = lax.axis_index("narrow") == lax.axis_size("narrow") - 1
    after_rows = jnp.where(is_final, following, shifted)
    weights_taps = pfb_window(FFT_LEN, TAPS).reshape(TAPS, 1, FFT_LEN)
    wb = jnp.broadcast_to(weights_taps, (TAPS, local_inputs, FFT_LEN))
    salt = lax.optimization_barrier(jnp.zeros((), jnp.int32))
    bh, bl = phase_matrices(salt)
    out = pfb_spectra(voltages, after_rows, wb, bh, bl)
    steps = local_spec // CHUNK
    c1_len = CHANNELS // PHASES
    out = out.reshape(steps, PHASES, 2, c1_len, local_inputs, CHUNK)
    spec = jnp.transpose(out, (3, 1, 2, 0, 4, 5))
    got = lax.all_to_all(spec, ("wide", "narrow"), 0, 0, tiled=True)
    return visibilities(got, lax.axis_size("narrow"))


def solution(mesh):
    in_specs = (P("wide", "narrow"), P("wide", None))
    out_specs = P(("wide", "narrow"), None, None, None)
    return jax.shard_map(shards, mesh=mesh, in_specs=in_specs, out_specs=out_specs, check_vma=False)
```

```python
import functools
import math

import jax
import jax.numpy as jnp
from jax import lax
from jax.experimental import pallas as pl
from jax.experimental.pallas import tpu as pltpu
from jax.sharding import PartitionSpec as P

FFT_LEN = 2048
CHANNELS = 1024
TAPS = 16
PHASES = 8
SUB_LEN = FFT_LEN // PHASES
CHUNK = 128


def from_behind(x, axis, by):
    size = lax.axis_size(axis)
    pairs = [(i, i + by) for i in range(size) if 0 <= i + by < size]
    return lax.ppermute(x, axis, pairs)


def pfb_window(block_len, tap_count):
    length_all = tap_count * block_len
    sample_pos = jnp.arange(length_all, dtype=jnp.float32)
    centred = (sample_pos + 0.5 - length_all / 2.0) / block_len
    taper = 0.5 - 0.5 * jnp.cos(2.0 * jnp.pi * (sample_pos + 0.5) / length_all)
    return jnp.sinc(centred) * taper


def phase_matrices(salt):
    k1 = jnp.arange(SUB_LEN, dtype=jnp.int32)[None, :, None]
    c1 = jnp.arange(CHANNELS // PHASES, dtype=jnp.int32)[None, None, :] + salt
    c2 = jnp.arange(PHASES, dtype=jnp.int32)[:, None, None]
    turns = (k1 * (PHASES * c1 + c2)) % FFT_LEN
    angles = (2.0 * jnp.pi / FFT_LEN) * turns.astype(jnp.float32)
    scaling = 1.0 / math.sqrt(FFT_LEN)
    cos_t = jnp.cos(angles) * scaling
    sin_t = jnp.sin(angles) * scaling
    top = jnp.concatenate([cos_t, -sin_t], axis=-1)
    bottom = jnp.concatenate([sin_t, cos_t], axis=-1)
    full = jnp.concatenate([top, bottom], axis=1)
    return split_exact(full)


def split_exact(value):
    scaled = value * 65537.0
    high = scaled - (scaled - value)
    low = value - high
    return high.astype(jnp.bfloat16), low.astype(jnp.bfloat16)


def split_parts(value):
    high = value.astype(jnp.bfloat16)
    low = (value - high.astype(jnp.float32)).astype(jnp.bfloat16)
    return high, low


def spectra_kernel(with_halo, *refs):
    if with_halo:
        xa_ref, xh_ref, wb_ref, bh_ref, bl_ref, _, out_ref, xf_ref, f_ref, uh_ref, ul_ref = refs
    else:
        xa_ref, wb_ref, bh_ref, bl_ref, out_ref, xf_ref, f_ref, uh_ref, ul_ref = refs
        xh_ref = xa_ref
    n_in = xa_ref.shape[0]
    own = CHUNK if with_halo else CHUNK + TAPS - 1

    def load_block(q_local, _):
        start = pl.multiple_of(q_local * FFT_LEN, FFT_LEN)
        xf_ref[q_local] = xa_ref[:, pl.ds(start, FFT_LEN)].astype(jnp.float32)
        return 0

    lax.fori_loop(0, own, load_block, 0)

    if with_halo:
        def body(j, _):
            start = pl.multiple_of(j * FFT_LEN, FFT_LEN)
            xf_ref[CHUNK + j] = xh_ref[:, pl.ds(start, FFT_LEN)].astype(jnp.float32)
            return 0
        lax.fori_loop(0, TAPS - 1, body, 0)

    lane_w = 128
    for lane_at in range(FFT_LEN // lane_w):
        lanes = slice(lane_at * lane_w, (lane_at + 1) * lane_w)
        taps = [wb_ref[p, :, lanes] for p in range(TAPS)]

        def filt(ml, _):
            terms = [taps[p] * xf_ref[ml + p, :, lanes] for p in range(TAPS)]
            while len(terms) > 1:
                terms = [terms[j] + terms[j + 1] for j in range(0, len(terms), 2)]
            f_ref[lane_at, pl.ds(ml, n_in, stride=CHUNK), :] = terms[0]
            return 0

        lax.fori_loop(0, CHUNK, filt, 0, unroll=4)

    half = 1.0 / math.sqrt(2.0)
    rows_per = 16
    sub_rows = 256

    for sub in range((CHUNK * n_in) // sub_rows):

        def butterflies(g, _):
            row = pl.multiple_of(sub * sub_rows + g * rows_per, rows_per)
            local = pl.multiple_of(g * rows_per, rows_per)
            rs = pl.ds(row, rows_per)
            ls = pl.ds(local, rows_per)
            for h in range(2):
                a = [f_ref[2 * n + h, rs, :] for n in range(PHASES)]
                s04 = a[0] + a[4]
                d04 = a[0] - a[4]
                s26 = a[2] + a[6]
                d26 = a[2] - a[6]
                s15 = a[1] + a[5]
                d15 = a[1] - a[5]
                s37 = a[3] + a[7]
                d37 = a[3] - a[7]
                e0 = s04 + s26
                e2 = s04 - s26
                o0 = s15 + s37
                o2 = s15 - s37
                p = half * (d15 - d37)
                q = half * (d15 + d37)
                outs = [
                    (e0 + o0, None),
                    (d04 + p, -d26 - q),
                    (e2, -o2),
                    (d04 - p, d26 - q),
                    (e0 - o0, None),
                    (d04 - p, -d26 + q),
                    (e2, o2),
                    (d04 + p, d26 + q),
                ]
                re_l = slice(h * 128, (h + 1) * 128)
                im_l = slice(SUB_LEN + h * 128, SUB_LEN + (h + 1) * 128)
                for c2, (re, im) in enumerate(outs):
                    hi, lo = split_parts(re)
                    uh_ref[c2, ls, re_l] = hi
                    ul_ref[c2, ls, re_l] = lo
                    if im is not None:
                        hi, lo = split_parts(im)
                        uh_ref[c2, ls, im_l] = hi
                        ul_ref[c2, ls, im_l] = lo
            return 0

        lax.fori_loop(0, sub_rows // rows_per, butterflies, 0)

        for c2 in range(PHASES):
            depth = SUB_LEN if c2 in (0, PHASES // 2) else 2 * SUB_LEN
            uh = uh_ref[c2, :, 0:depth]
            ul = ul_ref[c2, :, 0:depth]
            bh = bh_ref[c2, 0:depth, :]
            bl = bl_ref[c2, 0:depth, :]
            acc = jnp.dot(uh, bh, preferred_element_type=jnp.float32)
            acc = acc + jnp.dot(ul, bh, preferred_element_type=jnp.float32)
            acc = acc + jnp.dot(uh, bl, preferred_element_type=jnp.float32)
            out_ref[0, c2, :, sub * sub_rows:(sub + 1) * sub_rows] = acc.T.astype(jnp.bfloat16)


def pfb_chunk(xa, xh, wb, bh, bl, chunk_at, prev):
    n_in, span = xa.shape
    rows = CHUNK * n_in
    with_halo = xh is not None
    lanes = CHUNK * FFT_LEN if with_halo else (CHUNK + TAPS - 1) * FFT_LEN
    flops = 2 * rows * 3 * SUB_LEN * 2 * SUB_LEN * 7 + 2 * n_in * CHUNK * FFT_LEN * TAPS
    bytes_accessed = n_in * lanes * 2 + PHASES * rows * 2 * SUB_LEN * 2
    xa_spec = pl.BlockSpec((n_in, lanes), lambda s: (0, chunk_at))
    const3 = lambda s: (0, 0, 0)
    in_specs = [pl.BlockSpec(xa_spec.block_shape, xa_spec.index_map, pipeline_mode=pl.Buffered(1))]
    operands = [xa]
    if with_halo:
        in_specs.append(pl.BlockSpec(xh.shape, lambda s: (0, 0), pipeline_mode=pl.Buffered(1)))
        operands.append(xh)
    for arr in (wb, bh, bl):
        in_specs.append(pl.BlockSpec(arr.shape, const3, pipeline_mode=pl.Buffered(1)))
        operands.append(arr)
    aliases = {}
    if with_halo:
        in_specs.append(pl.BlockSpec(memory_space=pl.ANY))
        operands.append(prev)
        aliases = {len(operands) - 1: 0}
    steps = span // FFT_LEN // CHUNK
    return pl.pallas_call(
        functools.partial(spectra_kernel, with_halo),
        out_shape=jax.ShapeDtypeStruct((steps, PHASES, 2 * CHANNELS // PHASES, rows), jnp.bfloat16),
        grid=(1,),
        in_specs=in_specs,
        out_specs=pl.BlockSpec((1, PHASES, 2 * CHANNELS // PHASES, rows), lambda s: (chunk_at, 0, 0, 0)),
        input_output_aliases=aliases,
        scratch_shapes=[
            pltpu.VMEM((CHUNK + TAPS - 1, n_in, FFT_LEN), jnp.float32),
            pltpu.VMEM((FFT_LEN // 128, rows, 128), jnp.float32),
            pltpu.VMEM((PHASES, 256, 2 * SUB_LEN), jnp.bfloat16),
            pltpu.VMEM((PHASES, 256, 2 * SUB_LEN), jnp.bfloat16),
        ],
        compiler_params=pltpu.CompilerParams(
            dimension_semantics=("arbitrary",), vmem_limit_bytes=62 * 1024 * 1024
        ),
        cost_estimate=pl.CostEstimate(flops=flops, transcendentals=0, bytes_accessed=bytes_accessed),
    )(*operands)


def pfb_spectra(xa, xh, wb, bh, bl):
    n_spec = xa.shape[1] // FFT_LEN
    steps = n_spec // CHUNK
    first = pfb_chunk(xa, None, wb, bh, bl, 0, None)
    return pfb_chunk(xa, xh, wb, bh, bl, steps - 1, first)


def exchange_kernel(n_narrow, src_ref, dst_ref, send_sem, recv_sem, own_sem):
    n_dev = src_ref.shape[0]
    me = lax.axis_index("wide") * n_narrow + lax.axis_index("narrow")
    own = pltpu.make_async_copy(src_ref.at[me], dst_ref.at[me], own_sem)
    own.start()

    def send(k, _):
        peer = lax.rem(me + k, n_dev)
        pltpu.make_async_remote_copy(
            src_ref=src_ref.at[peer],
            dst_ref=dst_ref.at[me],
            send_sem=send_sem,
            recv_sem=recv_sem,
            device_id=(peer // n_narrow, peer % n_narrow),
            device_id_type=pl.DeviceIdType.MESH,
        ).start()
        return 0

    lax.fori_loop(1, n_dev, send, 0)
    own.wait()
    every = pltpu.make_async_remote_copy(
        src_ref=src_ref.at[pl.ds(0, n_dev - 1)],
        dst_ref=dst_ref.at[pl.ds(0, n_dev - 1)],
        send_sem=send_sem,
        recv_sem=recv_sem,
        device_id=(0, 0),
        device_id_type=pl.DeviceIdType.MESH,
    )
    every.wait_send()
    every.wait_recv()


def exchange(spec, n_narrow):
    return pl.pallas_call(
        functools.partial(exchange_kernel, n_narrow),
        out_shape=jax.ShapeDtypeStruct(spec.shape, spec.dtype),
        in_specs=[pl.BlockSpec(memory_space=pl.ANY)],
        out_specs=pl.BlockSpec(memory_space=pl.ANY),
        scratch_shapes=[pltpu.SemaphoreType.DMA(()), pltpu.SemaphoreType.DMA(()), pltpu.SemaphoreType.DMA(())],
        compiler_params=pltpu.CompilerParams(has_side_effects=True),
    )(spec)


def gram_kernel(n_narrow, g_ref, out_ref, l_ref):
    n_src = g_ref.shape[0]
    steps = g_ref.shape[3]
    seg = g_ref.shape[5]
    n_in = g_ref.shape[4]

    def gather(w, _):
        row = pl.multiple_of(w * n_in, n_in)
        for n in range(n_narrow):
            for ri in range(2):
                for s in range(steps):
                    col = ((ri * n_narrow + n) * steps + s) * seg
                    l_ref[pl.ds(row, n_in), col:col + seg] = g_ref[w * n_narrow + n, 0, ri, s].astype(jnp.float32)
        return 0

    lax.fori_loop(0, n_src // n_narrow, gather, 0)
    both = l_ref[...].astype(jnp.bfloat16)
    half = both.shape[1] // 2
    turned = jnp.concatenate([both[:, half:], -both[:, :half]], axis=1)
    nt = (((1,), (1,)), ((), ()))
    scale = 1.0 / half
    out_ref[0, 0] = lax.dot_general(both, both, nt, preferred_element_type=jnp.float32) * scale
    out_ref[0, 1] = lax.dot_general(turned, both, nt, preferred_element_type=jnp.float32) * scale


def visibilities(got, n_narrow):
    n_src, phases, parts, steps, n_in, seg = got.shape
    all_inputs = n_src // n_narrow * n_in
    depth = parts * n_narrow * steps * seg
    return pl.pallas_call(
        functools.partial(gram_kernel, n_narrow),
        out_shape=jax.ShapeDtypeStruct((phases, 2, all_inputs, all_inputs), jnp.float32),
        grid=(phases,),
        in_specs=[pl.BlockSpec((n_src, 1, parts, steps, n_in, seg), lambda c: (0, c, 0, 0, 0, 0))],
        out_specs=pl.BlockSpec((1, 2, all_inputs, all_inputs), lambda c: (c, 0, 0, 0)),
        scratch_shapes=[pltpu.VMEM((all_inputs, depth), jnp.float32)],
        compiler_params=pltpu.CompilerParams(
            dimension_semantics=("arbitrary",), vmem_limit_bytes=48 * 1024 * 1024
        ),
        cost_estimate=pl.CostEstimate(
            flops=phases * 4 * all_inputs * all_inputs * depth,
            transcendentals=0,
            bytes_accessed=got.size * 2 + phases * 2 * all_inputs * all_inputs * 4,
        ),
    )(got)


def shards(voltages, following):
    local_inputs, local_span = voltages.shape
    local_spec = local_span // FFT_LEN
    halo_len = (TAPS - 1) * FFT_LEN
    leading = voltages[:, :halo_len]
    shifted = from_behind(leading, "narrow", -1)
    is_final = lax.axis_index("narrow") == lax.axis_size("narrow") - 1
    after_rows = jnp.where(is_final, following, shifted)
    weights_taps = pfb_window(FFT_LEN, TAPS).reshape(TAPS, 1, FFT_LEN)
    wb = jnp.broadcast_to(weights_taps, (TAPS, local_inputs, FFT_LEN))
    salt = lax.optimization_barrier(jnp.zeros((), jnp.int32))
    bh, bl = phase_matrices(salt)
    out = pfb_spectra(voltages, after_rows, wb, bh, bl)
    steps = local_spec // CHUNK
    c1_len = CHANNELS // PHASES
    out = out.reshape(steps, PHASES, 2, c1_len, local_inputs, CHUNK)
    spec = jnp.transpose(out, (3, 1, 2, 0, 4, 5))
    got = exchange(spec, lax.axis_size("narrow"))
    return visibilities(got, lax.axis_size("narrow"))


def solution(mesh):
    in_specs = (P("wide", "narrow"), P("wide", None))
    out_specs = P(("wide", "narrow"), None, None, None)
    return jax.shard_map(shards, mesh=mesh, in_specs=in_specs, out_specs=out_specs, check_vma=False)
```

```python
import functools
import math

import jax
import jax.numpy as jnp
from jax import lax
from jax.experimental import pallas as pl
from jax.experimental.pallas import tpu as pltpu
from jax.sharding import PartitionSpec as P

FFT_LEN = 2048
CHANNELS = 1024
TAPS = 16
PHASES = 8
SUB_LEN = FFT_LEN // PHASES
CHUNK = 128


def from_behind(x, axis, by):
    size = lax.axis_size(axis)
    pairs = [(i, i + by) for i in range(size) if 0 <= i + by < size]
    return lax.ppermute(x, axis, pairs)


def pfb_window(block_len, tap_count):
    length_all = tap_count * block_len
    sample_pos = jnp.arange(length_all, dtype=jnp.float32)
    centred = (sample_pos + 0.5 - length_all / 2.0) / block_len
    taper = 0.5 - 0.5 * jnp.cos(2.0 * jnp.pi * (sample_pos + 0.5) / length_all)
    return jnp.sinc(centred) * taper


def phase_matrices(salt):
    c1 = jnp.arange(CHANNELS // PHASES, dtype=jnp.int32)[None, None, :] + salt
    c2 = jnp.arange(PHASES, dtype=jnp.int32)[:, None, None]
    chan = PHASES * c1 + c2
    step = 16
    a = jnp.arange(SUB_LEN // step, dtype=jnp.int32)[None, :, None]
    b = jnp.arange(step, dtype=jnp.int32)[None, :, None]
    coarse = (2.0 * jnp.pi / FFT_LEN) * ((a * step * chan) % FFT_LEN).astype(jnp.float32)
    fine = (2.0 * jnp.pi / FFT_LEN) * ((b * chan) % FFT_LEN).astype(jnp.float32)
    cc, sc = jnp.cos(coarse)[:, :, None, :], jnp.sin(coarse)[:, :, None, :]
    cf, sf = jnp.cos(fine)[:, None, :, :], jnp.sin(fine)[:, None, :, :]
    scaling = 1.0 / math.sqrt(FFT_LEN)
    shape = (PHASES, SUB_LEN, CHANNELS // PHASES)
    cos_t = ((cc * cf - sc * sf) * scaling).reshape(shape)
    sin_t = ((sc * cf + cc * sf) * scaling).reshape(shape)
    top = jnp.concatenate([cos_t, -sin_t], axis=-1)
    bottom = jnp.concatenate([sin_t, cos_t], axis=-1)
    full = jnp.concatenate([top, bottom], axis=1)
    return split_exact(full)


def split_exact(value):
    scaled = value * 65537.0
    high = scaled - (scaled - value)
    low = value - high
    return high.astype(jnp.bfloat16), low.astype(jnp.bfloat16)


def split_parts(value):
    high = value.astype(jnp.bfloat16)
    low = (value - high.astype(jnp.float32)).astype(jnp.bfloat16)
    return high, low


def spectra_kernel(with_halo, *refs):
    if with_halo:
        xa_ref, xh_ref, wb_ref, bh_ref, bl_ref, _, out_ref, xf_ref, f_ref, uh_ref, ul_ref = refs
    else:
        xa_ref, wb_ref, bh_ref, bl_ref, out_ref, xf_ref, f_ref, uh_ref, ul_ref = refs
        xh_ref = xa_ref
    n_in = xa_ref.shape[0]
    own = CHUNK if with_halo else CHUNK + TAPS - 1

    def load_block(q_local, _):
        start = pl.multiple_of(q_local * FFT_LEN, FFT_LEN)
        xf_ref[q_local] = xa_ref[:, pl.ds(start, FFT_LEN)].astype(jnp.float32)
        return 0

    lax.fori_loop(0, own, load_block, 0, unroll=4)

    if with_halo:
        def body(j, _):
            start = pl.multiple_of(j * FFT_LEN, FFT_LEN)
            xf_ref[CHUNK + j] = xh_ref[:, pl.ds(start, FFT_LEN)].astype(jnp.float32)
            return 0
        lax.fori_loop(0, TAPS - 1, body, 0, unroll=3)

    lane_w = 128
    for lane_at in range(FFT_LEN // lane_w):
        lanes = slice(lane_at * lane_w, (lane_at + 1) * lane_w)
        taps = [wb_ref[p, :, lanes] for p in range(TAPS)]

        def filt(ml, _):
            terms = [taps[p] * xf_ref[ml + p, :, lanes] for p in range(TAPS)]
            while len(terms) > 1:
                terms = [terms[j] + terms[j + 1] for j in range(0, len(terms), 2)]
            f_ref[lane_at, pl.ds(ml, n_in, stride=CHUNK), :] = terms[0]
            return 0

        lax.fori_loop(0, CHUNK, filt, 0, unroll=4)

    half = 1.0 / math.sqrt(2.0)
    rows_per = 16
    sub_rows = 256

    for sub in range((CHUNK * n_in) // sub_rows):

        def butterflies(g, _):
            row = pl.multiple_of(sub * sub_rows + g * rows_per, rows_per)
            local = pl.multiple_of(g * rows_per, rows_per)
            rs = pl.ds(row, rows_per)
            ls = pl.ds(local, rows_per)
            for h in range(2):
                a = [f_ref[2 * n + h, rs, :] for n in range(PHASES)]
                s04 = a[0] + a[4]
                d04 = a[0] - a[4]
                s26 = a[2] + a[6]
                d26 = a[2] - a[6]
                s15 = a[1] + a[5]
                d15 = a[1] - a[5]
                s37 = a[3] + a[7]
                d37 = a[3] - a[7]
                e0 = s04 + s26
                e2 = s04 - s26
                o0 = s15 + s37
                o2 = s15 - s37
                p = half * (d15 - d37)
                q = half * (d15 + d37)
                outs = [
                    (e0 + o0, None),
                    (d04 + p, -d26 - q),
                    (e2, -o2),
                    (d04 - p, d26 - q),
                    (e0 - o0, None),
                    (d04 - p, -d26 + q),
                    (e2, o2),
                    (d04 + p, d26 + q),
                ]
                re_l = slice(h * 128, (h + 1) * 128)
                im_l = slice(SUB_LEN + h * 128, SUB_LEN + (h + 1) * 128)
                for c2, (re, im) in enumerate(outs):
                    hi, lo = split_parts(re)
                    uh_ref[c2, ls, re_l] = hi
                    ul_ref[c2, ls, re_l] = lo
                    if im is not None:
                        hi, lo = split_parts(im)
                        uh_ref[c2, ls, im_l] = hi
                        ul_ref[c2, ls, im_l] = lo
            return 0

        lax.fori_loop(0, sub_rows // rows_per, butterflies, 0)

        for c2 in range(PHASES):
            depth = SUB_LEN if c2 in (0, PHASES // 2) else 2 * SUB_LEN
            uh = uh_ref[c2, :, 0:depth]
            ul = ul_ref[c2, :, 0:depth]
            bh = bh_ref[c2, 0:depth, :]
            bl = bl_ref[c2, 0:depth, :]
            acc = jnp.dot(uh, bh, preferred_element_type=jnp.float32)
            acc = acc + jnp.dot(ul, bh, preferred_element_type=jnp.float32)
            acc = acc + jnp.dot(uh, bl, preferred_element_type=jnp.float32)
            out_ref[0, c2, :, sub * sub_rows:(sub + 1) * sub_rows] = acc.T.astype(jnp.bfloat16)


def pfb_chunk(xa, xh, wb, bh, bl, chunk_at, prev):
    n_in, span = xa.shape
    rows = CHUNK * n_in
    with_halo = xh is not None
    lanes = CHUNK * FFT_LEN if with_halo else (CHUNK + TAPS - 1) * FFT_LEN
    flops = 2 * rows * 3 * SUB_LEN * 2 * SUB_LEN * 7 + 2 * n_in * CHUNK * FFT_LEN * TAPS
    bytes_accessed = n_in * lanes * 2 + PHASES * rows * 2 * SUB_LEN * 2
    xa_spec = pl.BlockSpec((n_in, lanes), lambda s: (0, chunk_at))
    const3 = lambda s: (0, 0, 0)
    in_specs = [pl.BlockSpec(xa_spec.block_shape, xa_spec.index_map, pipeline_mode=pl.Buffered(1))]
    operands = [xa]
    if with_halo:
        in_specs.append(pl.BlockSpec(xh.shape, lambda s: (0, 0), pipeline_mode=pl.Buffered(1)))
        operands.append(xh)
    for arr in (wb, bh, bl):
        in_specs.append(pl.BlockSpec(arr.shape, const3, pipeline_mode=pl.Buffered(1)))
        operands.append(arr)
    aliases = {}
    if with_halo:
        in_specs.append(pl.BlockSpec(memory_space=pl.ANY))
        operands.append(prev)
        aliases = {len(operands) - 1: 0}
    steps = span // FFT_LEN // CHUNK
    return pl.pallas_call(
        functools.partial(spectra_kernel, with_halo),
        out_shape=jax.ShapeDtypeStruct((steps, PHASES, 2 * CHANNELS // PHASES, rows), jnp.bfloat16),
        grid=(1,),
        in_specs=in_specs,
        out_specs=pl.BlockSpec((1, PHASES, 2 * CHANNELS // PHASES, rows), lambda s: (chunk_at, 0, 0, 0)),
        input_output_aliases=aliases,
        scratch_shapes=[
            pltpu.VMEM((CHUNK + TAPS - 1, n_in, FFT_LEN), jnp.float32),
            pltpu.VMEM((FFT_LEN // 128, rows, 128), jnp.float32),
            pltpu.VMEM((PHASES, 256, 2 * SUB_LEN), jnp.bfloat16),
            pltpu.VMEM((PHASES, 256, 2 * SUB_LEN), jnp.bfloat16),
        ],
        compiler_params=pltpu.CompilerParams(
            dimension_semantics=("arbitrary",), vmem_limit_bytes=62 * 1024 * 1024
        ),
        cost_estimate=pl.CostEstimate(flops=flops, transcendentals=0, bytes_accessed=bytes_accessed),
    )(*operands)


def pfb_spectra(xa, xh, wb, bh, bl):
    n_spec = xa.shape[1] // FFT_LEN
    steps = n_spec // CHUNK
    first = pfb_chunk(xa, None, wb, bh, bl, 0, None)
    return pfb_chunk(xa, xh, wb, bh, bl, steps - 1, first)


def gram_kernel(n_narrow, g_ref, out_ref, l_ref):
    n_src = g_ref.shape[0]
    steps = g_ref.shape[3]
    seg = g_ref.shape[5]
    n_in = g_ref.shape[4]

    def gather(w, _):
        row = pl.multiple_of(w * n_in, n_in)
        for n in range(n_narrow):
            for ri in range(2):
                for s in range(steps):
                    col = ((ri * n_narrow + n) * steps + s) * seg
                    l_ref[pl.ds(row, n_in), col:col + seg] = g_ref[w * n_narrow + n, 0, ri, s].astype(jnp.float32)
        return 0

    lax.fori_loop(0, n_src // n_narrow, gather, 0)
    both = l_ref[...].astype(jnp.bfloat16)
    half = both.shape[1] // 2
    turned = jnp.concatenate([both[:, half:], -both[:, :half]], axis=1)
    nt = (((1,), (1,)), ((), ()))
    scale = 1.0 / half
    out_ref[0, 0] = lax.dot_general(both, both, nt, preferred_element_type=jnp.float32) * scale
    out_ref[0, 1] = lax.dot_general(turned, both, nt, preferred_element_type=jnp.float32) * scale


def visibilities(got, n_narrow):
    n_src, phases, parts, steps, n_in, seg = got.shape
    all_inputs = n_src // n_narrow * n_in
    depth = parts * n_narrow * steps * seg
    return pl.pallas_call(
        functools.partial(gram_kernel, n_narrow),
        out_shape=jax.ShapeDtypeStruct((phases, 2, all_inputs, all_inputs), jnp.float32),
        grid=(phases,),
        in_specs=[pl.BlockSpec((n_src, 1, parts, steps, n_in, seg), lambda c: (0, c, 0, 0, 0, 0))],
        out_specs=pl.BlockSpec((1, 2, all_inputs, all_inputs), lambda c: (c, 0, 0, 0)),
        scratch_shapes=[pltpu.VMEM((all_inputs, depth), jnp.float32)],
        compiler_params=pltpu.CompilerParams(
            dimension_semantics=("arbitrary",), vmem_limit_bytes=48 * 1024 * 1024
        ),
        cost_estimate=pl.CostEstimate(
            flops=phases * 4 * all_inputs * all_inputs * depth,
            transcendentals=0,
            bytes_accessed=got.size * 2 + phases * 2 * all_inputs * all_inputs * 4,
        ),
    )(got)


def shards(voltages, following):
    local_inputs, local_span = voltages.shape
    local_spec = local_span // FFT_LEN
    halo_len = (TAPS - 1) * FFT_LEN
    leading = voltages[:, :halo_len]
    shifted = from_behind(leading, "narrow", -1)
    is_final = lax.axis_index("narrow") == lax.axis_size("narrow") - 1
    after_rows = jnp.where(is_final, following, shifted)
    weights_taps = pfb_window(FFT_LEN, TAPS).reshape(TAPS, 1, FFT_LEN)
    wb = jnp.broadcast_to(weights_taps, (TAPS, local_inputs, FFT_LEN))
    salt = lax.optimization_barrier(jnp.zeros((), jnp.int32))
    bh, bl = phase_matrices(salt)
    out = pfb_spectra(voltages, after_rows, wb, bh, bl)
    steps = local_spec // CHUNK
    c1_len = CHANNELS // PHASES
    out = out.reshape(steps, PHASES, 2, c1_len, local_inputs, CHUNK)
    spec = jnp.transpose(out, (3, 1, 2, 0, 4, 5))
    got = lax.all_to_all(spec, ("wide", "narrow"), 0, 0, tiled=True)
    return visibilities(got, lax.axis_size("narrow"))


def solution(mesh):
    in_specs = (P("wide", "narrow"), P("wide", None))
    out_specs = P(("wide", "narrow"), None, None, None)
    return jax.shard_map(shards, mesh=mesh, in_specs=in_specs, out_specs=out_specs, check_vma=False)
```

```python
import functools
import math

import jax
import jax.numpy as jnp
from jax import lax
from jax.experimental import pallas as pl
from jax.experimental.pallas import tpu as pltpu
from jax.sharding import PartitionSpec as P

FFT_LEN = 2048
CHANNELS = 1024
TAPS = 16
PHASES = 8
SUB_LEN = FFT_LEN // PHASES
CHUNK = 128


def from_behind(x, axis, by):
    size = lax.axis_size(axis)
    pairs = [(i, i + by) for i in range(size) if 0 <= i + by < size]
    return lax.ppermute(x, axis, pairs)


def pfb_window(block_len, tap_count):
    length_all = tap_count * block_len
    sample_pos = jnp.arange(length_all, dtype=jnp.float32)
    centred = (sample_pos + 0.5 - length_all / 2.0) / block_len
    taper = 0.5 - 0.5 * jnp.cos(2.0 * jnp.pi * (sample_pos + 0.5) / length_all)
    return jnp.sinc(centred) * taper


def phase_matrices(salt):
    c1 = jnp.arange(CHANNELS // PHASES, dtype=jnp.int32)[None, None, :] + salt
    c2 = jnp.arange(PHASES, dtype=jnp.int32)[:, None, None]
    chan = PHASES * c1 + c2
    step = 16
    a = jnp.arange(SUB_LEN // step, dtype=jnp.int32)[None, :, None]
    b = jnp.arange(step, dtype=jnp.int32)[None, :, None]
    coarse = (2.0 * jnp.pi / FFT_LEN) * ((a * step * chan) % FFT_LEN).astype(jnp.float32)
    fine = (2.0 * jnp.pi / FFT_LEN) * ((b * chan) % FFT_LEN).astype(jnp.float32)
    cc, sc = jnp.cos(coarse)[:, :, None, :], jnp.sin(coarse)[:, :, None, :]
    cf, sf = jnp.cos(fine)[:, None, :, :], jnp.sin(fine)[:, None, :, :]
    scaling = 1.0 / math.sqrt(FFT_LEN)
    shape = (PHASES, SUB_LEN, CHANNELS // PHASES)
    cos_t = ((cc * cf - sc * sf) * scaling).reshape(shape)
    sin_t = ((sc * cf + cc * sf) * scaling).reshape(shape)
    top = jnp.concatenate([cos_t, -sin_t], axis=-1)
    bottom = jnp.concatenate([sin_t, cos_t], axis=-1)
    full = jnp.concatenate([top, bottom], axis=1)
    return split_exact(full)


def split_exact(value):
    scaled = value * 65537.0
    high = scaled - (scaled - value)
    low = value - high
    return high.astype(jnp.bfloat16), low.astype(jnp.bfloat16)


def split_parts(value):
    high = value.astype(jnp.bfloat16)
    low = (value - high.astype(jnp.float32)).astype(jnp.bfloat16)
    return high, low


def spectra_kernel(with_halo, *refs):
    if with_halo:
        xa_ref, fol_ref, sh_ref, wb_ref, bh_ref, bl_ref, _, out_ref, xf_ref, f_ref, uh_ref, ul_ref = refs
    else:
        xa_ref, wb_ref, bh_ref, bl_ref, out_ref, xf_ref, f_ref, uh_ref, ul_ref = refs
    n_in = xa_ref.shape[0]
    own = CHUNK if with_halo else CHUNK + TAPS - 1

    def load_block(q_local, _):
        start = pl.multiple_of(q_local * FFT_LEN, FFT_LEN)
        xf_ref[q_local] = xa_ref[:, pl.ds(start, FFT_LEN)].astype(jnp.float32)
        return 0

    lax.fori_loop(0, own, load_block, 0, unroll=4)

    if with_halo:
        is_final = lax.axis_index("narrow") == lax.axis_size("narrow") - 1

        def body(j, _):
            start = pl.multiple_of(j * FFT_LEN, FFT_LEN)
            lanes = pl.ds(start, FFT_LEN)
            picked = jnp.where(is_final, fol_ref[:, lanes], sh_ref[:, lanes])
            xf_ref[CHUNK + j] = picked.astype(jnp.float32)
            return 0
        lax.fori_loop(0, TAPS - 1, body, 0, unroll=3)

    lane_w = 128
    for lane_at in range(FFT_LEN // lane_w):
        lanes = slice(lane_at * lane_w, (lane_at + 1) * lane_w)
        taps = [wb_ref[p, :, lanes] for p in range(TAPS)]

        def filt(ml, _):
            terms = [taps[p] * xf_ref[ml + p, :, lanes] for p in range(TAPS)]
            while len(terms) > 1:
                terms = [terms[j] + terms[j + 1] for j in range(0, len(terms), 2)]
            f_ref[lane_at, pl.ds(ml, n_in, stride=CHUNK), :] = terms[0]
            return 0

        lax.fori_loop(0, CHUNK, filt, 0, unroll=4)

    half = 1.0 / math.sqrt(2.0)
    rows_per = 16
    sub_rows = 256

    for sub in range((CHUNK * n_in) // sub_rows):

        def butterflies(g, _):
            row = pl.multiple_of(sub * sub_rows + g * rows_per, rows_per)
            local = pl.multiple_of(g * rows_per, rows_per)
            rs = pl.ds(row, rows_per)
            ls = pl.ds(local, rows_per)
            for h in range(2):
                a = [f_ref[2 * n + h, rs, :] for n in range(PHASES)]
                s04 = a[0] + a[4]
                d04 = a[0] - a[4]
                s26 = a[2] + a[6]
                d26 = a[2] - a[6]
                s15 = a[1] + a[5]
                d15 = a[1] - a[5]
                s37 = a[3] + a[7]
                d37 = a[3] - a[7]
                e0 = s04 + s26
                e2 = s04 - s26
                o0 = s15 + s37
                o2 = s15 - s37
                p = half * (d15 - d37)
                q = half * (d15 + d37)
                outs = [
                    (e0 + o0, None),
                    (d04 + p, -d26 - q),
                    (e2, -o2),
                    (d04 - p, d26 - q),
                    (e0 - o0, None),
                    (d04 - p, -d26 + q),
                    (e2, o2),
                    (d04 + p, d26 + q),
                ]
                re_l = slice(h * 128, (h + 1) * 128)
                im_l = slice(SUB_LEN + h * 128, SUB_LEN + (h + 1) * 128)
                for c2, (re, im) in enumerate(outs):
                    hi, lo = split_parts(re)
                    uh_ref[c2, ls, re_l] = hi
                    ul_ref[c2, ls, re_l] = lo
                    if im is not None:
                        hi, lo = split_parts(im)
                        uh_ref[c2, ls, im_l] = hi
                        ul_ref[c2, ls, im_l] = lo
            return 0

        lax.fori_loop(0, sub_rows // rows_per, butterflies, 0)

        for c2 in range(PHASES):
            depth = SUB_LEN if c2 in (0, PHASES // 2) else 2 * SUB_LEN
            uh = uh_ref[c2, :, 0:depth]
            ul = ul_ref[c2, :, 0:depth]
            bh = bh_ref[c2, 0:depth, :]
            bl = bl_ref[c2, 0:depth, :]
            acc = jnp.dot(uh, bh, preferred_element_type=jnp.float32)
            acc = acc + jnp.dot(ul, bh, preferred_element_type=jnp.float32)
            acc = acc + jnp.dot(uh, bl, preferred_element_type=jnp.float32)
            out_ref[0, c2, :, sub * sub_rows:(sub + 1) * sub_rows] = acc.T.astype(jnp.bfloat16)


def pfb_chunk(xa, xh, wb, bh, bl, chunk_at, prev):
    n_in, span = xa.shape
    rows = CHUNK * n_in
    with_halo = xh is not None
    lanes = CHUNK * FFT_LEN if with_halo else (CHUNK + TAPS - 1) * FFT_LEN
    flops = 2 * rows * 3 * SUB_LEN * 2 * SUB_LEN * 7 + 2 * n_in * CHUNK * FFT_LEN * TAPS
    bytes_accessed = n_in * lanes * 2 + PHASES * rows * 2 * SUB_LEN * 2
    xa_spec = pl.BlockSpec((n_in, lanes), lambda s: (0, chunk_at))
    const3 = lambda s: (0, 0, 0)
    in_specs = [pl.BlockSpec(xa_spec.block_shape, xa_spec.index_map, pipeline_mode=pl.Buffered(1))]
    operands = [xa]
    if with_halo:
        for arr in xh:
            in_specs.append(pl.BlockSpec(arr.shape, lambda s: (0, 0), pipeline_mode=pl.Buffered(1)))
            operands.append(arr)
    for arr in (wb, bh, bl):
        in_specs.append(pl.BlockSpec(arr.shape, const3, pipeline_mode=pl.Buffered(1)))
        operands.append(arr)
    aliases = {}
    if with_halo:
        in_specs.append(pl.BlockSpec(memory_space=pl.ANY))
        operands.append(prev)
        aliases = {len(operands) - 1: 0}
    steps = span // FFT_LEN // CHUNK
    return pl.pallas_call(
        functools.partial(spectra_kernel, with_halo),
        out_shape=jax.ShapeDtypeStruct((steps, PHASES, 2 * CHANNELS // PHASES, rows), jnp.bfloat16),
        grid=(1,),
        in_specs=in_specs,
        out_specs=pl.BlockSpec((1, PHASES, 2 * CHANNELS // PHASES, rows), lambda s: (chunk_at, 0, 0, 0)),
        input_output_aliases=aliases,
        scratch_shapes=[
            pltpu.VMEM((CHUNK + TAPS - 1, n_in, FFT_LEN), jnp.float32),
            pltpu.VMEM((FFT_LEN // 128, rows, 128), jnp.float32),
            pltpu.VMEM((PHASES, 256, 2 * SUB_LEN), jnp.bfloat16),
            pltpu.VMEM((PHASES, 256, 2 * SUB_LEN), jnp.bfloat16),
        ],
        compiler_params=pltpu.CompilerParams(
            dimension_semantics=("arbitrary",), vmem_limit_bytes=62 * 1024 * 1024
        ),
        cost_estimate=pl.CostEstimate(flops=flops, transcendentals=0, bytes_accessed=bytes_accessed),
    )(*operands)


def pfb_spectra(xa, xh, wb, bh, bl):
    n_spec = xa.shape[1] // FFT_LEN
    steps = n_spec // CHUNK
    first = pfb_chunk(xa, None, wb, bh, bl, 0, None)
    return pfb_chunk(xa, xh, wb, bh, bl, steps - 1, first)


def gram_kernel(n_narrow, g_ref, out_ref, l_ref):
    n_src = g_ref.shape[0]
    steps = g_ref.shape[3]
    seg = g_ref.shape[5]
    n_in = g_ref.shape[4]

    def gather(w, _):
        row = pl.multiple_of(w * n_in, n_in)
        for n in range(n_narrow):
            for ri in range(2):
                for s in range(steps):
                    col = ((ri * n_narrow + n) * steps + s) * seg
                    l_ref[pl.ds(row, n_in), col:col + seg] = g_ref[w * n_narrow + n, 0, ri, s].astype(jnp.float32)
        return 0

    lax.fori_loop(0, n_src // n_narrow, gather, 0)
    both = l_ref[...].astype(jnp.bfloat16)
    half = both.shape[1] // 2
    turned = jnp.concatenate([both[:, half:], -both[:, :half]], axis=1)
    nt = (((1,), (1,)), ((), ()))
    scale = 1.0 / half
    out_ref[0, 0] = lax.dot_general(both, both, nt, preferred_element_type=jnp.float32) * scale
    out_ref[0, 1] = lax.dot_general(turned, both, nt, preferred_element_type=jnp.float32) * scale


def visibilities(got, n_narrow):
    n_src, phases, parts, steps, n_in, seg = got.shape
    all_inputs = n_src // n_narrow * n_in
    depth = parts * n_narrow * steps * seg
    return pl.pallas_call(
        functools.partial(gram_kernel, n_narrow),
        out_shape=jax.ShapeDtypeStruct((phases, 2, all_inputs, all_inputs), jnp.float32),
        grid=(phases,),
        in_specs=[pl.BlockSpec((n_src, 1, parts, steps, n_in, seg), lambda c: (0, c, 0, 0, 0, 0))],
        out_specs=pl.BlockSpec((1, 2, all_inputs, all_inputs), lambda c: (c, 0, 0, 0)),
        scratch_shapes=[pltpu.VMEM((all_inputs, depth), jnp.float32)],
        compiler_params=pltpu.CompilerParams(
            dimension_semantics=("arbitrary",), vmem_limit_bytes=48 * 1024 * 1024
        ),
        cost_estimate=pl.CostEstimate(
            flops=phases * 4 * all_inputs * all_inputs * depth,
            transcendentals=0,
            bytes_accessed=got.size * 2 + phases * 2 * all_inputs * all_inputs * 4,
        ),
    )(got)


def shards(voltages, following):
    local_inputs, local_span = voltages.shape
    local_spec = local_span // FFT_LEN
    halo_len = (TAPS - 1) * FFT_LEN
    leading = voltages[:, :halo_len]
    shifted = from_behind(leading, "narrow", -1)
    after_rows = (following, shifted)
    weights_taps = pfb_window(FFT_LEN, TAPS).reshape(TAPS, 1, FFT_LEN)
    wb = jnp.broadcast_to(weights_taps, (TAPS, local_inputs, FFT_LEN))
    salt = lax.optimization_barrier(jnp.zeros((), jnp.int32))
    bh, bl = phase_matrices(salt)
    out = pfb_spectra(voltages, after_rows, wb, bh, bl)
    steps = local_spec // CHUNK
    c1_len = CHANNELS // PHASES
    out = out.reshape(steps, PHASES, 2, c1_len, local_inputs, CHUNK)
    spec = jnp.transpose(out, (3, 1, 2, 0, 4, 5))
    got = lax.all_to_all(spec, ("wide", "narrow"), 0, 0, tiled=True)
    return visibilities(got, lax.axis_size("narrow"))


def solution(mesh):
    in_specs = (P("wide", "narrow"), P("wide", None))
    out_specs = P(("wide", "narrow"), None, None, None)
    return jax.shard_map(shards, mesh=mesh, in_specs=in_specs, out_specs=out_specs, check_vma=False)
```

```python
import functools
import math

import jax
import jax.numpy as jnp
from jax import lax
from jax.experimental import pallas as pl
from jax.experimental.pallas import tpu as pltpu
from jax.sharding import PartitionSpec as P

FFT_LEN = 2048
CHANNELS = 1024
TAPS = 16
PHASES = 8
SUB_LEN = FFT_LEN // PHASES
CHUNK = 128


def from_behind(x, axis, by):
    size = lax.axis_size(axis)
    pairs = [(i, i + by) for i in range(size) if 0 <= i + by < size]
    return lax.ppermute(x, axis, pairs)


def pfb_window(block_len, tap_count):
    length_all = tap_count * block_len
    sample_pos = jnp.arange(length_all, dtype=jnp.float32)
    centred = (sample_pos + 0.5 - length_all / 2.0) / block_len
    taper = 0.5 - 0.5 * jnp.cos(2.0 * jnp.pi * (sample_pos + 0.5) / length_all)
    return jnp.sinc(centred) * taper


def phase_matrices(salt):
    c1 = jnp.arange(CHANNELS // PHASES, dtype=jnp.int32)[None, None, :] + salt
    c2 = jnp.arange(PHASES, dtype=jnp.int32)[:, None, None]
    chan = PHASES * c1 + c2
    step = 16
    a = jnp.arange(SUB_LEN // step, dtype=jnp.int32)[None, :, None]
    b = jnp.arange(step, dtype=jnp.int32)[None, :, None]
    coarse = (2.0 * jnp.pi / FFT_LEN) * ((a * step * chan) % FFT_LEN).astype(jnp.float32)
    fine = (2.0 * jnp.pi / FFT_LEN) * ((b * chan) % FFT_LEN).astype(jnp.float32)
    cc, sc = jnp.cos(coarse)[:, :, None, :], jnp.sin(coarse)[:, :, None, :]
    cf, sf = jnp.cos(fine)[:, None, :, :], jnp.sin(fine)[:, None, :, :]
    scaling = 1.0 / math.sqrt(FFT_LEN)
    shape = (PHASES, SUB_LEN, CHANNELS // PHASES)
    cos_t = ((cc * cf - sc * sf) * scaling).reshape(shape)
    sin_t = ((sc * cf + cc * sf) * scaling).reshape(shape)
    top = jnp.concatenate([cos_t, -sin_t], axis=-1)
    bottom = jnp.concatenate([sin_t, cos_t], axis=-1)
    full = jnp.concatenate([top, bottom], axis=1)
    return split_exact(full)


def split_exact(value):
    scaled = value * 65537.0
    high = scaled - (scaled - value)
    low = value - high
    return high.astype(jnp.bfloat16), low.astype(jnp.bfloat16)


def split_parts(value):
    high = value.astype(jnp.bfloat16)
    low = (value - high.astype(jnp.float32)).astype(jnp.bfloat16)
    return high, low


def spectra_kernel(with_halo, *refs):
    if with_halo:
        xa_ref, fol_ref, sh_ref, wb_ref, bh_ref, bl_ref, _, out_ref, xf_ref, f_ref, uh_ref, ul_ref = refs
    else:
        xa_ref, wb_ref, bh_ref, bl_ref, out_ref, xf_ref, f_ref, uh_ref, ul_ref = refs
    n_in = xa_ref.shape[0]
    own = CHUNK if with_halo else CHUNK + TAPS - 1

    def load_block(q_local, _):
        start = pl.multiple_of(q_local * FFT_LEN, FFT_LEN)
        xf_ref[q_local] = xa_ref[:, pl.ds(start, FFT_LEN)].astype(jnp.float32)
        return 0

    lax.fori_loop(0, own, load_block, 0, unroll=4)

    if with_halo:
        is_final = lax.axis_index("narrow") == lax.axis_size("narrow") - 1

        def body(j, _):
            start = pl.multiple_of(j * FFT_LEN, FFT_LEN)
            lanes = pl.ds(start, FFT_LEN)
            picked = jnp.where(is_final, fol_ref[:, lanes], sh_ref[:, lanes])
            xf_ref[CHUNK + j] = picked.astype(jnp.float32)
            return 0
        lax.fori_loop(0, TAPS - 1, body, 0, unroll=3)

    lane_w = 128
    for lane_at in range(FFT_LEN // lane_w):
        lanes = slice(lane_at * lane_w, (lane_at + 1) * lane_w)
        taps = [wb_ref[p, :, lanes] for p in range(TAPS)]

        def filt(ml, _):
            terms = [taps[p] * xf_ref[ml + p, :, lanes] for p in range(TAPS)]
            while len(terms) > 1:
                terms = [terms[j] + terms[j + 1] for j in range(0, len(terms), 2)]
            f_ref[lane_at, pl.ds(ml, n_in, stride=CHUNK), :] = terms[0]
            return 0

        lax.fori_loop(0, CHUNK, filt, 0, unroll=4)

    half = 1.0 / math.sqrt(2.0)
    rows_per = 16
    sub_rows = 256

    for sub in range((CHUNK * n_in) // sub_rows):

        def butterflies(g, _):
            row = pl.multiple_of(sub * sub_rows + g * rows_per, rows_per)
            local = pl.multiple_of(g * rows_per, rows_per)
            rs = pl.ds(row, rows_per)
            ls = pl.ds(local, rows_per)
            for h in range(2):
                a = [f_ref[2 * n + h, rs, :] for n in range(PHASES)]
                s04 = a[0] + a[4]
                d04 = a[0] - a[4]
                s26 = a[2] + a[6]
                d26 = a[2] - a[6]
                s15 = a[1] + a[5]
                d15 = a[1] - a[5]
                s37 = a[3] + a[7]
                d37 = a[3] - a[7]
                e0 = s04 + s26
                e2 = s04 - s26
                o0 = s15 + s37
                o2 = s15 - s37
                p = half * (d15 - d37)
                q = half * (d15 + d37)
                outs = [
                    (e0 + o0, None),
                    (d04 + p, -d26 - q),
                    (e2, -o2),
                    (d04 - p, d26 - q),
                    (e0 - o0, None),
                    (d04 - p, -d26 + q),
                    (e2, o2),
                    (d04 + p, d26 + q),
                ]
                re_l = slice(h * 128, (h + 1) * 128)
                im_l = slice(SUB_LEN + h * 128, SUB_LEN + (h + 1) * 128)
                for c2, (re, im) in enumerate(outs):
                    hi, lo = split_parts(re)
                    uh_ref[c2, ls, re_l] = hi
                    ul_ref[c2, ls, re_l] = lo
                    if im is not None:
                        hi, lo = split_parts(im)
                        uh_ref[c2, ls, im_l] = hi
                        ul_ref[c2, ls, im_l] = lo
            return 0

        lax.fori_loop(0, sub_rows // rows_per, butterflies, 0)

        for c2 in range(PHASES):
            depth = SUB_LEN if c2 in (0, PHASES // 2) else 2 * SUB_LEN
            uh = uh_ref[c2, :, 0:depth]
            ul = ul_ref[c2, :, 0:depth]
            bh = bh_ref[c2, 0:depth, :]
            bl = bl_ref[c2, 0:depth, :]
            acc = jnp.dot(uh, bh, preferred_element_type=jnp.float32)
            acc = acc + jnp.dot(ul, bh, preferred_element_type=jnp.float32)
            acc = acc + jnp.dot(uh, bl, preferred_element_type=jnp.float32)
            out_ref[0, c2, :, sub * sub_rows:(sub + 1) * sub_rows] = acc.T.astype(jnp.bfloat16)


def pfb_chunk(xa, xh, wb, bh, bl, chunk_at, prev):
    n_in, span = xa.shape
    rows = CHUNK * n_in
    with_halo = xh is not None
    lanes = CHUNK * FFT_LEN if with_halo else (CHUNK + TAPS - 1) * FFT_LEN
    flops = 2 * rows * 3 * SUB_LEN * 2 * SUB_LEN * 7 + 2 * n_in * CHUNK * FFT_LEN * TAPS
    bytes_accessed = n_in * lanes * 2 + PHASES * rows * 2 * SUB_LEN * 2
    xa_spec = pl.BlockSpec((n_in, lanes), lambda s: (0, chunk_at))
    const3 = lambda s: (0, 0, 0)
    in_specs = [pl.BlockSpec(xa_spec.block_shape, xa_spec.index_map, pipeline_mode=pl.Buffered(1))]
    operands = [xa]
    if with_halo:
        for arr in xh:
            in_specs.append(pl.BlockSpec(arr.shape, lambda s: (0, 0), pipeline_mode=pl.Buffered(1)))
            operands.append(arr)
    for arr in (wb, bh, bl):
        in_specs.append(pl.BlockSpec(arr.shape, const3, pipeline_mode=pl.Buffered(1)))
        operands.append(arr)
    aliases = {}
    if with_halo:
        in_specs.append(pl.BlockSpec(memory_space=pl.ANY))
        operands.append(prev)
        aliases = {len(operands) - 1: 0}
    steps = span // FFT_LEN // CHUNK
    return pl.pallas_call(
        functools.partial(spectra_kernel, with_halo),
        out_shape=jax.ShapeDtypeStruct((steps, PHASES, 2 * CHANNELS // PHASES, rows), jnp.bfloat16),
        grid=(1,),
        in_specs=in_specs,
        out_specs=pl.BlockSpec((1, PHASES, 2 * CHANNELS // PHASES, rows), lambda s: (chunk_at, 0, 0, 0)),
        input_output_aliases=aliases,
        scratch_shapes=[
            pltpu.VMEM((CHUNK + TAPS - 1, n_in, FFT_LEN), jnp.float32),
            pltpu.VMEM((FFT_LEN // 128, rows, 128), jnp.float32),
            pltpu.VMEM((PHASES, 256, 2 * SUB_LEN), jnp.bfloat16),
            pltpu.VMEM((PHASES, 256, 2 * SUB_LEN), jnp.bfloat16),
        ],
        compiler_params=pltpu.CompilerParams(
            dimension_semantics=("arbitrary",), vmem_limit_bytes=62 * 1024 * 1024
        ),
        cost_estimate=pl.CostEstimate(flops=flops, transcendentals=0, bytes_accessed=bytes_accessed),
    )(*operands)


def pfb_spectra(xa, xh, wb, bh, bl):
    n_spec = xa.shape[1] // FFT_LEN
    steps = n_spec // CHUNK
    first = pfb_chunk(xa, None, wb, bh, bl, 0, None)
    return pfb_chunk(xa, xh, wb, bh, bl, steps - 1, first)


def gram_kernel(n_narrow, g_ref, out_ref, l_ref):
    n_src = g_ref.shape[0]
    steps = g_ref.shape[3]
    seg = g_ref.shape[5]
    n_in = g_ref.shape[4]

    def gather(w, _):
        row = pl.multiple_of(w * n_in, n_in)
        for n in range(n_narrow):
            for ri in range(2):
                for s in range(steps):
                    col = ((ri * n_narrow + n) * steps + s) * seg
                    l_ref[pl.ds(row, n_in), col:col + seg] = g_ref[w * n_narrow + n, 0, ri, s].astype(jnp.float32)
        return 0

    lax.fori_loop(0, n_src // n_narrow, gather, 0)
    rows = l_ref[...]
    both = rows.astype(jnp.bfloat16)
    both_t = rows.T.astype(jnp.bfloat16)
    half = both.shape[1] // 2
    turned = jnp.concatenate([both[:, half:], -both[:, :half]], axis=1)
    scale = 1.0 / half
    out_ref[0, 0] = jnp.dot(both, both_t, preferred_element_type=jnp.float32) * scale
    out_ref[0, 1] = jnp.dot(turned, both_t, preferred_element_type=jnp.float32) * scale


def visibilities(got, n_narrow):
    n_src, phases, parts, steps, n_in, seg = got.shape
    all_inputs = n_src // n_narrow * n_in
    depth = parts * n_narrow * steps * seg
    return pl.pallas_call(
        functools.partial(gram_kernel, n_narrow),
        out_shape=jax.ShapeDtypeStruct((phases, 2, all_inputs, all_inputs), jnp.float32),
        grid=(phases,),
        in_specs=[pl.BlockSpec((n_src, 1, parts, steps, n_in, seg), lambda c: (0, c, 0, 0, 0, 0))],
        out_specs=pl.BlockSpec((1, 2, all_inputs, all_inputs), lambda c: (c, 0, 0, 0)),
        scratch_shapes=[pltpu.VMEM((all_inputs, depth), jnp.float32)],
        compiler_params=pltpu.CompilerParams(
            dimension_semantics=("arbitrary",), vmem_limit_bytes=48 * 1024 * 1024
        ),
        cost_estimate=pl.CostEstimate(
            flops=phases * 4 * all_inputs * all_inputs * depth,
            transcendentals=0,
            bytes_accessed=got.size * 2 + phases * 2 * all_inputs * all_inputs * 4,
        ),
    )(got)


def shards(voltages, following):
    local_inputs, local_span = voltages.shape
    local_spec = local_span // FFT_LEN
    halo_len = (TAPS - 1) * FFT_LEN
    leading = voltages[:, :halo_len]
    shifted = from_behind(leading, "narrow", -1)
    after_rows = (following, shifted)
    weights_taps = pfb_window(FFT_LEN, TAPS).reshape(TAPS, 1, FFT_LEN)
    wb = jnp.broadcast_to(weights_taps, (TAPS, local_inputs, FFT_LEN))
    salt = lax.optimization_barrier(jnp.zeros((), jnp.int32))
    bh, bl = phase_matrices(salt)
    out = pfb_spectra(voltages, after_rows, wb, bh, bl)
    steps = local_spec // CHUNK
    c1_len = CHANNELS // PHASES
    out = out.reshape(steps, PHASES, 2, c1_len, local_inputs, CHUNK)
    spec = jnp.transpose(out, (3, 1, 2, 0, 4, 5))
    got = lax.all_to_all(spec, ("wide", "narrow"), 0, 0, tiled=True)
    return visibilities(got, lax.axis_size("narrow"))


def solution(mesh):
    in_specs = (P("wide", "narrow"), P("wide", None))
    out_specs = P(("wide", "narrow"), None, None, None)
    return jax.shard_map(shards, mesh=mesh, in_specs=in_specs, out_specs=out_specs, check_vma=False)
```

```python
import functools
import math

import jax
import jax.numpy as jnp
from jax import lax
from jax.experimental import pallas as pl
from jax.experimental.pallas import tpu as pltpu
from jax.sharding import PartitionSpec as P

FFT_LEN = 2048
CHANNELS = 1024
TAPS = 16
PHASES = 8
SUB_LEN = FFT_LEN // PHASES
CHUNK = 128


def from_behind(x, axis, by):
    size = lax.axis_size(axis)
    pairs = [(i, i + by) for i in range(size) if 0 <= i + by < size]
    return lax.ppermute(x, axis, pairs)


def pfb_window(block_len, tap_count):
    length_all = tap_count * block_len
    sample_pos = jnp.arange(length_all, dtype=jnp.float32)
    centred = (sample_pos + 0.5 - length_all / 2.0) / block_len
    taper = 0.5 - 0.5 * jnp.cos(2.0 * jnp.pi * (sample_pos + 0.5) / length_all)
    return jnp.sinc(centred) * taper


def phase_matrices(salt):
    c1 = jnp.arange(CHANNELS // PHASES, dtype=jnp.int32)[None, None, :] + salt
    c2 = jnp.arange(PHASES, dtype=jnp.int32)[:, None, None]
    chan = PHASES * c1 + c2
    step = 16
    a = jnp.arange(SUB_LEN // step, dtype=jnp.int32)[None, :, None]
    b = jnp.arange(step, dtype=jnp.int32)[None, :, None]
    coarse = (2.0 * jnp.pi / FFT_LEN) * ((a * step * chan) % FFT_LEN).astype(jnp.float32)
    fine = (2.0 * jnp.pi / FFT_LEN) * ((b * chan) % FFT_LEN).astype(jnp.float32)
    cc, sc = jnp.cos(coarse)[:, :, None, :], jnp.sin(coarse)[:, :, None, :]
    cf, sf = jnp.cos(fine)[:, None, :, :], jnp.sin(fine)[:, None, :, :]
    scaling = 1.0 / math.sqrt(FFT_LEN)
    shape = (PHASES, SUB_LEN, CHANNELS // PHASES)
    cos_t = ((cc * cf - sc * sf) * scaling).reshape(shape)
    sin_t = ((sc * cf + cc * sf) * scaling).reshape(shape)
    top = jnp.concatenate([cos_t, -sin_t], axis=-1)
    bottom = jnp.concatenate([sin_t, cos_t], axis=-1)
    full = jnp.concatenate([top, bottom], axis=1)
    return split_exact(full)


def split_exact(value):
    scaled = value * 65537.0
    high = scaled - (scaled - value)
    low = value - high
    return high.astype(jnp.bfloat16), low.astype(jnp.bfloat16)


def split_parts(value):
    high = value.astype(jnp.bfloat16)
    low = (value - high.astype(jnp.float32)).astype(jnp.bfloat16)
    return high, low


def spectra_kernel(with_halo, *refs):
    if with_halo:
        xa_ref, fol_ref, sh_ref, wb_ref, bh_ref, bl_ref, _, out_ref, xf_ref, f_ref, uh_ref, ul_ref = refs
    else:
        xa_ref, wb_ref, bh_ref, bl_ref, out_ref, xf_ref, f_ref, uh_ref, ul_ref = refs
    n_in = xa_ref.shape[0]
    own = CHUNK if with_halo else CHUNK + TAPS - 1

    def load_block(q_local, _):
        start = pl.multiple_of(q_local * FFT_LEN, FFT_LEN)
        xf_ref[q_local] = xa_ref[:, pl.ds(start, FFT_LEN)].astype(jnp.float32)
        return 0

    lax.fori_loop(0, own, load_block, 0, unroll=4)

    if with_halo:
        is_final = lax.axis_index("narrow") == lax.axis_size("narrow") - 1

        def body(j, _):
            start = pl.multiple_of(j * FFT_LEN, FFT_LEN)
            lanes = pl.ds(start, FFT_LEN)
            picked = jnp.where(is_final, fol_ref[:, lanes], sh_ref[:, lanes])
            xf_ref[CHUNK + j] = picked.astype(jnp.float32)
            return 0
        lax.fori_loop(0, TAPS - 1, body, 0, unroll=3)

    lane_w = 128
    for lane_at in range(FFT_LEN // lane_w):
        lanes = slice(lane_at * lane_w, (lane_at + 1) * lane_w)
        taps = [wb_ref[p, :, lanes] for p in range(TAPS)]

        def filt(ml, _):
            terms = [taps[p] * xf_ref[ml + p, :, lanes] for p in range(TAPS)]
            while len(terms) > 1:
                terms = [terms[j] + terms[j + 1] for j in range(0, len(terms), 2)]
            f_ref[lane_at, pl.ds(ml, n_in, stride=CHUNK), :] = terms[0]
            return 0

        lax.fori_loop(0, CHUNK, filt, 0, unroll=4)

    half = 1.0 / math.sqrt(2.0)
    rows_per = 16
    sub_rows = 256

    for sub in range((CHUNK * n_in) // sub_rows):

        def butterflies(g, _):
            row = pl.multiple_of(sub * sub_rows + g * rows_per, rows_per)
            local = pl.multiple_of(g * rows_per, rows_per)
            rs = pl.ds(row, rows_per)
            ls = pl.ds(local, rows_per)
            for h in range(2):
                a = [f_ref[2 * n + h, rs, :] for n in range(PHASES)]
                s04 = a[0] + a[4]
                d04 = a[0] - a[4]
                s26 = a[2] + a[6]
                d26 = a[2] - a[6]
                s15 = a[1] + a[5]
                d15 = a[1] - a[5]
                s37 = a[3] + a[7]
                d37 = a[3] - a[7]
                e0 = s04 + s26
                e2 = s04 - s26
                o0 = s15 + s37
                o2 = s15 - s37
                p = half * (d15 - d37)
                q = half * (d15 + d37)
                outs = [
                    (e0 + o0, None),
                    (d04 + p, -d26 - q),
                    (e2, -o2),
                    (d04 - p, d26 - q),
                    (e0 - o0, None),
                    (d04 - p, -d26 + q),
                    (e2, o2),
                    (d04 + p, d26 + q),
                ]
                re_l = slice(h * 128, (h + 1) * 128)
                im_l = slice(SUB_LEN + h * 128, SUB_LEN + (h + 1) * 128)
                for c2, (re, im) in enumerate(outs):
                    hi, lo = split_parts(re)
                    uh_ref[c2, ls, re_l] = hi
                    ul_ref[c2, ls, re_l] = lo
                    if im is not None:
                        hi, lo = split_parts(im)
                        uh_ref[c2, ls, im_l] = hi
                        ul_ref[c2, ls, im_l] = lo
            return 0

        lax.fori_loop(0, sub_rows // rows_per, butterflies, 0, unroll=2)

        for c2 in range(PHASES):
            depth = SUB_LEN if c2 in (0, PHASES // 2) else 2 * SUB_LEN
            uh = uh_ref[c2, :, 0:depth]
            ul = ul_ref[c2, :, 0:depth]
            bh = bh_ref[c2, 0:depth, :]
            bl = bl_ref[c2, 0:depth, :]
            acc = jnp.dot(uh, bh, preferred_element_type=jnp.float32)
            acc = acc + jnp.dot(ul, bh, preferred_element_type=jnp.float32)
            acc = acc + jnp.dot(uh, bl, preferred_element_type=jnp.float32)
            out_ref[0, c2, :, sub * sub_rows:(sub + 1) * sub_rows] = acc.T.astype(jnp.bfloat16)


def pfb_chunk(xa, xh, wb, bh, bl, chunk_at, prev):
    n_in, span = xa.shape
    rows = CHUNK * n_in
    with_halo = xh is not None
    lanes = CHUNK * FFT_LEN if with_halo else (CHUNK + TAPS - 1) * FFT_LEN
    flops = 2 * rows * 3 * SUB_LEN * 2 * SUB_LEN * 7 + 2 * n_in * CHUNK * FFT_LEN * TAPS
    bytes_accessed = n_in * lanes * 2 + PHASES * rows * 2 * SUB_LEN * 2
    xa_spec = pl.BlockSpec((n_in, lanes), lambda s: (0, chunk_at))
    const3 = lambda s: (0, 0, 0)
    in_specs = [pl.BlockSpec(xa_spec.block_shape, xa_spec.index_map, pipeline_mode=pl.Buffered(1))]
    operands = [xa]
    if with_halo:
        for arr in xh:
            in_specs.append(pl.BlockSpec(arr.shape, lambda s: (0, 0), pipeline_mode=pl.Buffered(1)))
            operands.append(arr)
    for arr in (wb, bh, bl):
        in_specs.append(pl.BlockSpec(arr.shape, const3, pipeline_mode=pl.Buffered(1)))
        operands.append(arr)
    aliases = {}
    if with_halo:
        in_specs.append(pl.BlockSpec(memory_space=pl.ANY))
        operands.append(prev)
        aliases = {len(operands) - 1: 0}
    steps = span // FFT_LEN // CHUNK
    return pl.pallas_call(
        functools.partial(spectra_kernel, with_halo),
        out_shape=jax.ShapeDtypeStruct((steps, PHASES, 2 * CHANNELS // PHASES, rows), jnp.bfloat16),
        grid=(1,),
        in_specs=in_specs,
        out_specs=pl.BlockSpec((1, PHASES, 2 * CHANNELS // PHASES, rows), lambda s: (chunk_at, 0, 0, 0)),
        input_output_aliases=aliases,
        scratch_shapes=[
            pltpu.VMEM((CHUNK + TAPS - 1, n_in, FFT_LEN), jnp.float32),
            pltpu.VMEM((FFT_LEN // 128, rows, 128), jnp.float32),
            pltpu.VMEM((PHASES, 256, 2 * SUB_LEN), jnp.bfloat16),
            pltpu.VMEM((PHASES, 256, 2 * SUB_LEN), jnp.bfloat16),
        ],
        compiler_params=pltpu.CompilerParams(
            dimension_semantics=("arbitrary",), vmem_limit_bytes=62 * 1024 * 1024
        ),
        cost_estimate=pl.CostEstimate(flops=flops, transcendentals=0, bytes_accessed=bytes_accessed),
    )(*operands)


def pfb_spectra(xa, xh, wb, bh, bl):
    n_spec = xa.shape[1] // FFT_LEN
    steps = n_spec // CHUNK
    first = pfb_chunk(xa, None, wb, bh, bl, 0, None)
    return pfb_chunk(xa, xh, wb, bh, bl, steps - 1, first)


def gram_kernel(n_narrow, g_ref, out_ref, l_ref):
    n_src = g_ref.shape[0]
    steps = g_ref.shape[3]
    seg = g_ref.shape[5]
    n_in = g_ref.shape[4]

    def gather(w, _):
        row = pl.multiple_of(w * n_in, n_in)
        for n in range(n_narrow):
            for ri in range(2):
                for s in range(steps):
                    col = ((ri * n_narrow + n) * steps + s) * seg
                    l_ref[pl.ds(row, n_in), col:col + seg] = g_ref[w * n_narrow + n, 0, ri, s].astype(jnp.float32)
        return 0

    lax.fori_loop(0, n_src // n_narrow, gather, 0, unroll=2)
    both = l_ref[...].astype(jnp.bfloat16)
    half = both.shape[1] // 2
    turned = jnp.concatenate([both[:, half:], -both[:, :half]], axis=1)
    nt = (((1,), (1,)), ((), ()))
    scale = 1.0 / half
    out_ref[0, 0] = lax.dot_general(both, both, nt, preferred_element_type=jnp.float32) * scale
    out_ref[0, 1] = lax.dot_general(turned, both, nt, preferred_element_type=jnp.float32) * scale


def visibilities(got, n_narrow):
    n_src, phases, parts, steps, n_in, seg = got.shape
    all_inputs = n_src // n_narrow * n_in
    depth = parts * n_narrow * steps * seg
    return pl.pallas_call(
        functools.partial(gram_kernel, n_narrow),
        out_shape=jax.ShapeDtypeStruct((phases, 2, all_inputs, all_inputs), jnp.float32),
        grid=(phases,),
        in_specs=[pl.BlockSpec((n_src, 1, parts, steps, n_in, seg), lambda c: (0, c, 0, 0, 0, 0))],
        out_specs=pl.BlockSpec((1, 2, all_inputs, all_inputs), lambda c: (c, 0, 0, 0)),
        scratch_shapes=[pltpu.VMEM((all_inputs, depth), jnp.float32)],
        compiler_params=pltpu.CompilerParams(
            dimension_semantics=("arbitrary",), vmem_limit_bytes=48 * 1024 * 1024
        ),
        cost_estimate=pl.CostEstimate(
            flops=phases * 4 * all_inputs * all_inputs * depth,
            transcendentals=0,
            bytes_accessed=got.size * 2 + phases * 2 * all_inputs * all_inputs * 4,
        ),
    )(got)


def shards(voltages, following):
    local_inputs, local_span = voltages.shape
    local_spec = local_span // FFT_LEN
    halo_len = (TAPS - 1) * FFT_LEN
    leading = voltages[:, :halo_len]
    shifted = from_behind(leading, "narrow", -1)
    after_rows = (following, shifted)
    weights_taps = pfb_window(FFT_LEN, TAPS).reshape(TAPS, 1, FFT_LEN)
    wb = jnp.broadcast_to(weights_taps, (TAPS, local_inputs, FFT_LEN))
    salt = lax.optimization_barrier(jnp.zeros((), jnp.int32))
    bh, bl = phase_matrices(salt)
    out = pfb_spectra(voltages, after_rows, wb, bh, bl)
    steps = local_spec // CHUNK
    c1_len = CHANNELS // PHASES
    out = out.reshape(steps, PHASES, 2, c1_len, local_inputs, CHUNK)
    spec = jnp.transpose(out, (3, 1, 2, 0, 4, 5))
    got = lax.all_to_all(spec, ("wide", "narrow"), 0, 0, tiled=True)
    return visibilities(got, lax.axis_size("narrow"))


def solution(mesh):
    in_specs = (P("wide", "narrow"), P("wide", None))
    out_specs = P(("wide", "narrow"), None, None, None)
    return jax.shard_map(shards, mesh=mesh, in_specs=in_specs, out_specs=out_specs, check_vma=False)
```

```python
import functools
import math

import jax
import jax.numpy as jnp
from jax import lax
from jax.experimental import pallas as pl
from jax.experimental.pallas import tpu as pltpu
from jax.sharding import PartitionSpec as P

FFT_LEN = 2048
CHANNELS = 1024
TAPS = 16
PHASES = 8
SUB_LEN = FFT_LEN // PHASES
CHUNK = 128


def from_behind(x, axis, by):
    size = lax.axis_size(axis)
    pairs = [(i, i + by) for i in range(size) if 0 <= i + by < size]
    return lax.ppermute(x, axis, pairs)


def pfb_window(block_len, tap_count):
    length_all = tap_count * block_len
    sample_pos = jnp.arange(length_all, dtype=jnp.float32)
    centred = (sample_pos + 0.5 - length_all / 2.0) / block_len
    taper = 0.5 - 0.5 * jnp.cos(2.0 * jnp.pi * (sample_pos + 0.5) / length_all)
    return jnp.sinc(centred) * taper


def phase_matrices(salt):
    c1 = jnp.arange(CHANNELS // PHASES, dtype=jnp.int32)[None, None, :] + salt
    c2 = jnp.arange(PHASES, dtype=jnp.int32)[:, None, None]
    chan = PHASES * c1 + c2
    step = 16
    a = jnp.arange(SUB_LEN // step, dtype=jnp.int32)[None, :, None]
    b = jnp.arange(step, dtype=jnp.int32)[None, :, None]
    coarse = (2.0 * jnp.pi / FFT_LEN) * ((a * step * chan) % FFT_LEN).astype(jnp.float32)
    fine = (2.0 * jnp.pi / FFT_LEN) * ((b * chan) % FFT_LEN).astype(jnp.float32)
    cc, sc = jnp.cos(coarse)[:, :, None, :], jnp.sin(coarse)[:, :, None, :]
    cf, sf = jnp.cos(fine)[:, None, :, :], jnp.sin(fine)[:, None, :, :]
    scaling = 1.0 / math.sqrt(FFT_LEN)
    shape = (PHASES, SUB_LEN, CHANNELS // PHASES)
    cos_t = ((cc * cf - sc * sf) * scaling).reshape(shape)
    sin_t = ((sc * cf + cc * sf) * scaling).reshape(shape)
    top = jnp.concatenate([cos_t, -sin_t], axis=-1)
    bottom = jnp.concatenate([sin_t, cos_t], axis=-1)
    full = jnp.concatenate([top, bottom], axis=1)
    return split_exact(full)


def split_exact(value):
    scaled = value * 65537.0
    high = scaled - (scaled - value)
    low = value - high
    return high.astype(jnp.bfloat16), low.astype(jnp.bfloat16)


def split_parts(value):
    high = value.astype(jnp.bfloat16)
    low = (value - high.astype(jnp.float32)).astype(jnp.bfloat16)
    return high, low


def spectra_kernel(with_halo, *refs):
    if with_halo:
        xa_ref, fol_ref, sh_ref, wb_ref, bh_ref, bl_ref, _, out_ref, xf_ref, f_ref, uh_ref, ul_ref = refs
    else:
        xa_ref, wb_ref, bh_ref, bl_ref, out_ref, xf_ref, f_ref, uh_ref, ul_ref = refs
    n_in = xa_ref.shape[0]
    own = CHUNK if with_halo else CHUNK + TAPS - 1

    def load_block(q_local, _):
        start = pl.multiple_of(q_local * FFT_LEN, FFT_LEN)
        xf_ref[q_local] = xa_ref[:, pl.ds(start, FFT_LEN)].astype(jnp.float32)
        return 0

    lax.fori_loop(0, own, load_block, 0, unroll=4)

    if with_halo:
        is_final = lax.axis_index("narrow") == lax.axis_size("narrow") - 1

        def body(j, _):
            start = pl.multiple_of(j * FFT_LEN, FFT_LEN)
            lanes = pl.ds(start, FFT_LEN)
            picked = jnp.where(is_final, fol_ref[:, lanes], sh_ref[:, lanes])
            xf_ref[CHUNK + j] = picked.astype(jnp.float32)
            return 0
        lax.fori_loop(0, TAPS - 1, body, 0, unroll=3)

    lane_w = 128
    for lane_at in range(FFT_LEN // lane_w):
        lanes = slice(lane_at * lane_w, (lane_at + 1) * lane_w)
        taps = [wb_ref[p, :, lanes] for p in range(TAPS)]

        def filt(ml, _):
            terms = [taps[p] * xf_ref[ml + p, :, lanes] for p in range(TAPS)]
            while len(terms) > 1:
                terms = [terms[j] + terms[j + 1] for j in range(0, len(terms), 2)]
            f_ref[lane_at, pl.ds(ml, n_in, stride=CHUNK), :] = terms[0]
            return 0

        lax.fori_loop(0, CHUNK, filt, 0, unroll=8)

    half = 1.0 / math.sqrt(2.0)
    rows_per = 16
    sub_rows = 256

    for sub in range((CHUNK * n_in) // sub_rows):

        def butterflies(g, _):
            row = pl.multiple_of(sub * sub_rows + g * rows_per, rows_per)
            local = pl.multiple_of(g * rows_per, rows_per)
            rs = pl.ds(row, rows_per)
            ls = pl.ds(local, rows_per)
            for h in range(2):
                a = [f_ref[2 * n + h, rs, :] for n in range(PHASES)]
                s04 = a[0] + a[4]
                d04 = a[0] - a[4]
                s26 = a[2] + a[6]
                d26 = a[2] - a[6]
                s15 = a[1] + a[5]
                d15 = a[1] - a[5]
                s37 = a[3] + a[7]
                d37 = a[3] - a[7]
                e0 = s04 + s26
                e2 = s04 - s26
                o0 = s15 + s37
                o2 = s15 - s37
                p = half * (d15 - d37)
                q = half * (d15 + d37)
                outs = [
                    (e0 + o0, None),
                    (d04 + p, -d26 - q),
                    (e2, -o2),
                    (d04 - p, d26 - q),
                    (e0 - o0, None),
                    (d04 - p, -d26 + q),
                    (e2, o2),
                    (d04 + p, d26 + q),
                ]
                re_l = slice(h * 128, (h + 1) * 128)
                im_l = slice(SUB_LEN + h * 128, SUB_LEN + (h + 1) * 128)
                for c2, (re, im) in enumerate(outs):
                    hi, lo = split_parts(re)
                    uh_ref[c2, ls, re_l] = hi
                    ul_ref[c2, ls, re_l] = lo
                    if im is not None:
                        hi, lo = split_parts(im)
                        uh_ref[c2, ls, im_l] = hi
                        ul_ref[c2, ls, im_l] = lo
            return 0

        lax.fori_loop(0, sub_rows // rows_per, butterflies, 0, unroll=2)

        for c2 in range(PHASES):
            depth = SUB_LEN if c2 in (0, PHASES // 2) else 2 * SUB_LEN
            uh = uh_ref[c2, :, 0:depth]
            ul = ul_ref[c2, :, 0:depth]
            bh = bh_ref[c2, 0:depth, :]
            bl = bl_ref[c2, 0:depth, :]
            acc = jnp.dot(uh, bh, preferred_element_type=jnp.float32)
            acc = acc + jnp.dot(ul, bh, preferred_element_type=jnp.float32)
            acc = acc + jnp.dot(uh, bl, preferred_element_type=jnp.float32)
            out_ref[0, c2, :, sub * sub_rows:(sub + 1) * sub_rows] = acc.T.astype(jnp.bfloat16)


def pfb_chunk(xa, xh, wb, bh, bl, chunk_at, prev):
    n_in, span = xa.shape
    rows = CHUNK * n_in
    with_halo = xh is not None
    lanes = CHUNK * FFT_LEN if with_halo else (CHUNK + TAPS - 1) * FFT_LEN
    flops = 2 * rows * 3 * SUB_LEN * 2 * SUB_LEN * 7 + 2 * n_in * CHUNK * FFT_LEN * TAPS
    bytes_accessed = n_in * lanes * 2 + PHASES * rows * 2 * SUB_LEN * 2
    xa_spec = pl.BlockSpec((n_in, lanes), lambda s: (0, chunk_at))
    const3 = lambda s: (0, 0, 0)
    in_specs = [pl.BlockSpec(xa_spec.block_shape, xa_spec.index_map, pipeline_mode=pl.Buffered(1))]
    operands = [xa]
    if with_halo:
        for arr in xh:
            in_specs.append(pl.BlockSpec(arr.shape, lambda s: (0, 0), pipeline_mode=pl.Buffered(1)))
            operands.append(arr)
    for arr in (wb, bh, bl):
        in_specs.append(pl.BlockSpec(arr.shape, const3, pipeline_mode=pl.Buffered(1)))
        operands.append(arr)
    aliases = {}
    if with_halo:
        in_specs.append(pl.BlockSpec(memory_space=pl.ANY))
        operands.append(prev)
        aliases = {len(operands) - 1: 0}
    steps = span // FFT_LEN // CHUNK
    return pl.pallas_call(
        functools.partial(spectra_kernel, with_halo),
        out_shape=jax.ShapeDtypeStruct((steps, PHASES, 2 * CHANNELS // PHASES, rows), jnp.bfloat16),
        grid=(1,),
        in_specs=in_specs,
        out_specs=pl.BlockSpec((1, PHASES, 2 * CHANNELS // PHASES, rows), lambda s: (chunk_at, 0, 0, 0)),
        input_output_aliases=aliases,
        scratch_shapes=[
            pltpu.VMEM((CHUNK + TAPS - 1, n_in, FFT_LEN), jnp.float32),
            pltpu.VMEM((FFT_LEN // 128, rows, 128), jnp.float32),
            pltpu.VMEM((PHASES, 256, 2 * SUB_LEN), jnp.bfloat16),
            pltpu.VMEM((PHASES, 256, 2 * SUB_LEN), jnp.bfloat16),
        ],
        compiler_params=pltpu.CompilerParams(
            dimension_semantics=("arbitrary",), vmem_limit_bytes=62 * 1024 * 1024
        ),
        cost_estimate=pl.CostEstimate(flops=flops, transcendentals=0, bytes_accessed=bytes_accessed),
    )(*operands)


def pfb_spectra(xa, xh, wb, bh, bl):
    n_spec = xa.shape[1] // FFT_LEN
    steps = n_spec // CHUNK
    first = pfb_chunk(xa, None, wb, bh, bl, 0, None)
    return pfb_chunk(xa, xh, wb, bh, bl, steps - 1, first)


def gram_kernel(n_narrow, g_ref, out_ref, l_ref):
    n_src = g_ref.shape[0]
    steps = g_ref.shape[3]
    seg = g_ref.shape[5]
    n_in = g_ref.shape[4]

    def gather(w, _):
        row = pl.multiple_of(w * n_in, n_in)
        for n in range(n_narrow):
            for ri in range(2):
                for s in range(steps):
                    col = ((ri * n_narrow + n) * steps + s) * seg
                    l_ref[pl.ds(row, n_in), col:col + seg] = g_ref[w * n_narrow + n, 0, ri, s].astype(jnp.float32)
        return 0

    lax.fori_loop(0, n_src // n_narrow, gather, 0, unroll=4)
    both = l_ref[...].astype(jnp.bfloat16)
    half = both.shape[1] // 2
    turned = jnp.concatenate([both[:, half:], -both[:, :half]], axis=1)
    nt = (((1,), (1,)), ((), ()))
    scale = 1.0 / half
    out_ref[0, 0] = lax.dot_general(both, both, nt, preferred_element_type=jnp.float32) * scale
    out_ref[0, 1] = lax.dot_general(turned, both, nt, preferred_element_type=jnp.float32) * scale


def visibilities(got, n_narrow):
    n_src, phases, parts, steps, n_in, seg = got.shape
    all_inputs = n_src // n_narrow * n_in
    depth = parts * n_narrow * steps * seg
    return pl.pallas_call(
        functools.partial(gram_kernel, n_narrow),
        out_shape=jax.ShapeDtypeStruct((phases, 2, all_inputs, all_inputs), jnp.float32),
        grid=(phases,),
        in_specs=[pl.BlockSpec((n_src, 1, parts, steps, n_in, seg), lambda c: (0, c, 0, 0, 0, 0))],
        out_specs=pl.BlockSpec((1, 2, all_inputs, all_inputs), lambda c: (c, 0, 0, 0)),
        scratch_shapes=[pltpu.VMEM((all_inputs, depth), jnp.float32)],
        compiler_params=pltpu.CompilerParams(
            dimension_semantics=("arbitrary",), vmem_limit_bytes=48 * 1024 * 1024
        ),
        cost_estimate=pl.CostEstimate(
            flops=phases * 4 * all_inputs * all_inputs * depth,
            transcendentals=0,
            bytes_accessed=got.size * 2 + phases * 2 * all_inputs * all_inputs * 4,
        ),
    )(got)


def shards(voltages, following):
    local_inputs, local_span = voltages.shape
    local_spec = local_span // FFT_LEN
    halo_len = (TAPS - 1) * FFT_LEN
    leading = voltages[:, :halo_len]
    shifted = from_behind(leading, "narrow", -1)
    after_rows = (following, shifted)
    weights_taps = pfb_window(FFT_LEN, TAPS).reshape(TAPS, 1, FFT_LEN)
    wb = jnp.broadcast_to(weights_taps, (TAPS, local_inputs, FFT_LEN))
    salt = lax.optimization_barrier(jnp.zeros((), jnp.int32))
    bh, bl = phase_matrices(salt)
    out = pfb_spectra(voltages, after_rows, wb, bh, bl)
    steps = local_spec // CHUNK
    c1_len = CHANNELS // PHASES
    out = out.reshape(steps, PHASES, 2, c1_len, local_inputs, CHUNK)
    spec = jnp.transpose(out, (3, 1, 2, 0, 4, 5))
    got = lax.all_to_all(spec, ("wide", "narrow"), 0, 0, tiled=True)
    return visibilities(got, lax.axis_size("narrow"))


def solution(mesh):
    in_specs = (P("wide", "narrow"), P("wide", None))
    out_specs = P(("wide", "narrow"), None, None, None)
    return jax.shard_map(shards, mesh=mesh, in_specs=in_specs, out_specs=out_specs, check_vma=False)
```

```python
import functools
import math

import jax
import jax.numpy as jnp
from jax import lax
from jax.experimental import pallas as pl
from jax.experimental.pallas import tpu as pltpu
from jax.sharding import PartitionSpec as P

FFT_LEN = 2048
CHANNELS = 1024
TAPS = 16
PHASES = 8
SUB_LEN = FFT_LEN // PHASES
CHUNK = 128


def from_behind(x, axis, by):
    size = lax.axis_size(axis)
    pairs = [(i, i + by) for i in range(size) if 0 <= i + by < size]
    return lax.ppermute(x, axis, pairs)


def pfb_window(block_len, tap_count):
    length_all = tap_count * block_len
    sample_pos = jnp.arange(length_all, dtype=jnp.float32)
    centred = (sample_pos + 0.5 - length_all / 2.0) / block_len
    taper = 0.5 - 0.5 * jnp.cos(2.0 * jnp.pi * (sample_pos + 0.5) / length_all)
    return jnp.sinc(centred) * taper


def phase_matrices(salt):
    c1 = jnp.arange(CHANNELS // PHASES, dtype=jnp.int32)[None, None, :] + salt
    c2 = jnp.arange(PHASES, dtype=jnp.int32)[:, None, None]
    chan = PHASES * c1 + c2
    step = 16
    a = jnp.arange(SUB_LEN // step, dtype=jnp.int32)[None, :, None]
    b = jnp.arange(step, dtype=jnp.int32)[None, :, None]
    coarse = (2.0 * jnp.pi / FFT_LEN) * ((a * step * chan) % FFT_LEN).astype(jnp.float32)
    fine = (2.0 * jnp.pi / FFT_LEN) * ((b * chan) % FFT_LEN).astype(jnp.float32)
    cc, sc = jnp.cos(coarse)[:, :, None, :], jnp.sin(coarse)[:, :, None, :]
    cf, sf = jnp.cos(fine)[:, None, :, :], jnp.sin(fine)[:, None, :, :]
    scaling = 1.0 / math.sqrt(FFT_LEN)
    shape = (PHASES, SUB_LEN, CHANNELS // PHASES)
    cos_t = ((cc * cf - sc * sf) * scaling).reshape(shape)
    sin_t = ((sc * cf + cc * sf) * scaling).reshape(shape)
    top = jnp.concatenate([cos_t, -sin_t], axis=-1)
    bottom = jnp.concatenate([sin_t, cos_t], axis=-1)
    full = jnp.concatenate([top, bottom], axis=1)
    return split_exact(full)


def split_exact(value):
    scaled = value * 65537.0
    high = scaled - (scaled - value)
    low = value - high
    return high.astype(jnp.bfloat16), low.astype(jnp.bfloat16)


def split_parts(value):
    high = value.astype(jnp.bfloat16)
    low = (value - high.astype(jnp.float32)).astype(jnp.bfloat16)
    return high, low


def spectra_kernel(with_halo, *refs):
    if with_halo:
        xa_ref, fol_ref, sh_ref, wb_ref, bh_ref, bl_ref, _, out_ref, xf_ref, f_ref, uh_ref, ul_ref = refs
    else:
        xa_ref, wb_ref, bh_ref, bl_ref, out_ref, xf_ref, f_ref, uh_ref, ul_ref = refs
    n_in = xa_ref.shape[0]
    own = CHUNK if with_halo else CHUNK + TAPS - 1

    def load_block(q_local, _):
        start = pl.multiple_of(q_local * FFT_LEN, FFT_LEN)
        xf_ref[q_local] = xa_ref[:, pl.ds(start, FFT_LEN)].astype(jnp.float32)
        return 0

    lax.fori_loop(0, own, load_block, 0, unroll=4)

    if with_halo:
        is_final = lax.axis_index("narrow") == lax.axis_size("narrow") - 1

        def body(j, _):
            start = pl.multiple_of(j * FFT_LEN, FFT_LEN)
            lanes = pl.ds(start, FFT_LEN)
            picked = jnp.where(is_final, fol_ref[:, lanes], sh_ref[:, lanes])
            xf_ref[CHUNK + j] = picked.astype(jnp.float32)
            return 0
        lax.fori_loop(0, TAPS - 1, body, 0, unroll=3)

    lane_w = 128
    for lane_at in range(FFT_LEN // lane_w):
        lanes = slice(lane_at * lane_w, (lane_at + 1) * lane_w)
        taps = [wb_ref[p, :, lanes] for p in range(TAPS)]

        def filt(ml, _):
            terms = [taps[p] * xf_ref[ml + p, :, lanes] for p in range(TAPS)]
            while len(terms) > 1:
                terms = [terms[j] + terms[j + 1] for j in range(0, len(terms), 2)]
            f_ref[lane_at, pl.ds(ml, n_in, stride=CHUNK), :] = terms[0]
            return 0

        lax.fori_loop(0, CHUNK, filt, 0, unroll=16)

    half = 1.0 / math.sqrt(2.0)
    rows_per = 16
    sub_rows = 256

    for sub in range((CHUNK * n_in) // sub_rows):

        def butterflies(g, _):
            row = pl.multiple_of(sub * sub_rows + g * rows_per, rows_per)
            local = pl.multiple_of(g * rows_per, rows_per)
            rs = pl.ds(row, rows_per)
            ls = pl.ds(local, rows_per)
            for h in range(2):
                a = [f_ref[2 * n + h, rs, :] for n in range(PHASES)]
                s04 = a[0] + a[4]
                d04 = a[0] - a[4]
                s26 = a[2] + a[6]
                d26 = a[2] - a[6]
                s15 = a[1] + a[5]
                d15 = a[1] - a[5]
                s37 = a[3] + a[7]
                d37 = a[3] - a[7]
                e0 = s04 + s26
                e2 = s04 - s26
                o0 = s15 + s37
                o2 = s15 - s37
                p = half * (d15 - d37)
                q = half * (d15 + d37)
                outs = [
                    (e0 + o0, None),
                    (d04 + p, -d26 - q),
                    (e2, -o2),
                    (d04 - p, d26 - q),
                    (e0 - o0, None),
                    (d04 - p, -d26 + q),
                    (e2, o2),
                    (d04 + p, d26 + q),
                ]
                re_l = slice(h * 128, (h + 1) * 128)
                im_l = slice(SUB_LEN + h * 128, SUB_LEN + (h + 1) * 128)
                for c2, (re, im) in enumerate(outs):
                    hi, lo = split_parts(re)
                    uh_ref[c2, ls, re_l] = hi
                    ul_ref[c2, ls, re_l] = lo
                    if im is not None:
                        hi, lo = split_parts(im)
                        uh_ref[c2, ls, im_l] = hi
                        ul_ref[c2, ls, im_l] = lo
            return 0

        lax.fori_loop(0, sub_rows // rows_per, butterflies, 0, unroll=2)

        for c2 in range(PHASES):
            depth = SUB_LEN if c2 in (0, PHASES // 2) else 2 * SUB_LEN
            uh = uh_ref[c2, :, 0:depth]
            ul = ul_ref[c2, :, 0:depth]
            bh = bh_ref[c2, 0:depth, :]
            bl = bl_ref[c2, 0:depth, :]
            acc = jnp.dot(uh, bh, preferred_element_type=jnp.float32)
            acc = acc + jnp.dot(ul, bh, preferred_element_type=jnp.float32)
            acc = acc + jnp.dot(uh, bl, preferred_element_type=jnp.float32)
            out_ref[0, c2, :, sub * sub_rows:(sub + 1) * sub_rows] = acc.T.astype(jnp.bfloat16)


def pfb_chunk(xa, xh, wb, bh, bl, chunk_at, prev):
    n_in, span = xa.shape
    rows = CHUNK * n_in
    with_halo = xh is not None
    lanes = CHUNK * FFT_LEN if with_halo else (CHUNK + TAPS - 1) * FFT_LEN
    flops = 2 * rows * 3 * SUB_LEN * 2 * SUB_LEN * 7 + 2 * n_in * CHUNK * FFT_LEN * TAPS
    bytes_accessed = n_in * lanes * 2 + PHASES * rows * 2 * SUB_LEN * 2
    xa_spec = pl.BlockSpec((n_in, lanes), lambda s: (0, chunk_at))
    const3 = lambda s: (0, 0, 0)
    in_specs = [pl.BlockSpec(xa_spec.block_shape, xa_spec.index_map, pipeline_mode=pl.Buffered(1))]
    operands = [xa]
    if with_halo:
        for arr in xh:
            in_specs.append(pl.BlockSpec(arr.shape, lambda s: (0, 0), pipeline_mode=pl.Buffered(1)))
            operands.append(arr)
    for arr in (wb, bh, bl):
        in_specs.append(pl.BlockSpec(arr.shape, const3, pipeline_mode=pl.Buffered(1)))
        operands.append(arr)
    aliases = {}
    if with_halo:
        in_specs.append(pl.BlockSpec(memory_space=pl.ANY))
        operands.append(prev)
        aliases = {len(operands) - 1: 0}
    steps = span // FFT_LEN // CHUNK
    return pl.pallas_call(
        functools.partial(spectra_kernel, with_halo),
        out_shape=jax.ShapeDtypeStruct((steps, PHASES, 2 * CHANNELS // PHASES, rows), jnp.bfloat16),
        grid=(1,),
        in_specs=in_specs,
        out_specs=pl.BlockSpec((1, PHASES, 2 * CHANNELS // PHASES, rows), lambda s: (chunk_at, 0, 0, 0)),
        input_output_aliases=aliases,
        scratch_shapes=[
            pltpu.VMEM((CHUNK + TAPS - 1, n_in, FFT_LEN), jnp.float32),
            pltpu.VMEM((FFT_LEN // 128, rows, 128), jnp.float32),
            pltpu.VMEM((PHASES, 256, 2 * SUB_LEN), jnp.bfloat16),
            pltpu.VMEM((PHASES, 256, 2 * SUB_LEN), jnp.bfloat16),
        ],
        compiler_params=pltpu.CompilerParams(
            dimension_semantics=("arbitrary",), vmem_limit_bytes=62 * 1024 * 1024
        ),
        cost_estimate=pl.CostEstimate(flops=flops, transcendentals=0, bytes_accessed=bytes_accessed),
    )(*operands)


def pfb_spectra(xa, xh, wb, bh, bl):
    n_spec = xa.shape[1] // FFT_LEN
    steps = n_spec // CHUNK
    first = pfb_chunk(xa, None, wb, bh, bl, 0, None)
    return pfb_chunk(xa, xh, wb, bh, bl, steps - 1, first)


def gram_kernel(n_narrow, g_ref, out_ref, l_ref):
    n_src = g_ref.shape[0]
    steps = g_ref.shape[3]
    seg = g_ref.shape[5]
    n_in = g_ref.shape[4]

    def gather(w, _):
        row = pl.multiple_of(w * n_in, n_in)
        for n in range(n_narrow):
            for ri in range(2):
                for s in range(steps):
                    col = ((ri * n_narrow + n) * steps + s) * seg
                    l_ref[pl.ds(row, n_in), col:col + seg] = g_ref[w * n_narrow + n, 0, ri, s].astype(jnp.float32)
        return 0

    lax.fori_loop(0, n_src // n_narrow, gather, 0, unroll=4)
    both = l_ref[...].astype(jnp.bfloat16)
    half = both.shape[1] // 2
    turned = jnp.concatenate([both[:, half:], -both[:, :half]], axis=1)
    nt = (((1,), (1,)), ((), ()))
    scale = 1.0 / half
    out_ref[0, 0] = lax.dot_general(both, both, nt, preferred_element_type=jnp.float32) * scale
    out_ref[0, 1] = lax.dot_general(turned, both, nt, preferred_element_type=jnp.float32) * scale


def visibilities(got, n_narrow):
    n_src, phases, parts, steps, n_in, seg = got.shape
    all_inputs = n_src // n_narrow * n_in
    depth = parts * n_narrow * steps * seg
    return pl.pallas_call(
        functools.partial(gram_kernel, n_narrow),
        out_shape=jax.ShapeDtypeStruct((phases, 2, all_inputs, all_inputs), jnp.float32),
        grid=(phases,),
        in_specs=[pl.BlockSpec((n_src, 1, parts, steps, n_in, seg), lambda c: (0, c, 0, 0, 0, 0))],
        out_specs=pl.BlockSpec((1, 2, all_inputs, all_inputs), lambda c: (c, 0, 0, 0)),
        scratch_shapes=[pltpu.VMEM((all_inputs, depth), jnp.float32)],
        compiler_params=pltpu.CompilerParams(
            dimension_semantics=("arbitrary",), vmem_limit_bytes=48 * 1024 * 1024
        ),
        cost_estimate=pl.CostEstimate(
            flops=phases * 4 * all_inputs * all_inputs * depth,
            transcendentals=0,
            bytes_accessed=got.size * 2 + phases * 2 * all_inputs * all_inputs * 4,
        ),
    )(got)


def shards(voltages, following):
    local_inputs, local_span = voltages.shape
    local_spec = local_span // FFT_LEN
    halo_len = (TAPS - 1) * FFT_LEN
    leading = voltages[:, :halo_len]
    shifted = from_behind(leading, "narrow", -1)
    after_rows = (following, shifted)
    weights_taps = pfb_window(FFT_LEN, TAPS).reshape(TAPS, 1, FFT_LEN)
    wb = jnp.broadcast_to(weights_taps, (TAPS, local_inputs, FFT_LEN))
    salt = lax.optimization_barrier(jnp.zeros((), jnp.int32))
    bh, bl = phase_matrices(salt)
    out = pfb_spectra(voltages, after_rows, wb, bh, bl)
    steps = local_spec // CHUNK
    c1_len = CHANNELS // PHASES
    out = out.reshape(steps, PHASES, 2, c1_len, local_inputs, CHUNK)
    spec = jnp.transpose(out, (3, 1, 2, 0, 4, 5))
    got = lax.all_to_all(spec, ("wide", "narrow"), 0, 0, tiled=True)
    return visibilities(got, lax.axis_size("narrow"))


def solution(mesh):
    in_specs = (P("wide", "narrow"), P("wide", None))
    out_specs = P(("wide", "narrow"), None, None, None)
    return jax.shard_map(shards, mesh=mesh, in_specs=in_specs, out_specs=out_specs, check_vma=False)
```

```python
import functools
import math

import jax
import jax.numpy as jnp
from jax import lax
from jax.experimental import pallas as pl
from jax.experimental.pallas import tpu as pltpu
from jax.sharding import PartitionSpec as P

FFT_LEN = 2048
CHANNELS = 1024
TAPS = 16
PHASES = 8
SUB_LEN = FFT_LEN // PHASES
CHUNK = 128


def from_behind(x, axis, by):
    size = lax.axis_size(axis)
    pairs = [(i, i + by) for i in range(size) if 0 <= i + by < size]
    return lax.ppermute(x, axis, pairs)


def pfb_window(block_len, tap_count):
    length_all = tap_count * block_len
    sample_pos = jnp.arange(length_all, dtype=jnp.float32)
    centred = (sample_pos + 0.5 - length_all / 2.0) / block_len
    taper = 0.5 - 0.5 * jnp.cos(2.0 * jnp.pi * (sample_pos + 0.5) / length_all)
    return jnp.sinc(centred) * taper


def phase_matrices(salt):
    c1 = jnp.arange(CHANNELS // PHASES, dtype=jnp.int32)[None, None, :] + salt
    c2 = jnp.arange(PHASES, dtype=jnp.int32)[:, None, None]
    chan = PHASES * c1 + c2
    step = 16
    a = jnp.arange(SUB_LEN // step, dtype=jnp.int32)[None, :, None]
    b = jnp.arange(step, dtype=jnp.int32)[None, :, None]
    coarse = (2.0 * jnp.pi / FFT_LEN) * ((a * step * chan) % FFT_LEN).astype(jnp.float32)
    fine = (2.0 * jnp.pi / FFT_LEN) * ((b * chan) % FFT_LEN).astype(jnp.float32)
    cc, sc = jnp.cos(coarse)[:, :, None, :], jnp.sin(coarse)[:, :, None, :]
    cf, sf = jnp.cos(fine)[:, None, :, :], jnp.sin(fine)[:, None, :, :]
    scaling = 1.0 / math.sqrt(FFT_LEN)
    shape = (PHASES, SUB_LEN, CHANNELS // PHASES)
    cos_t = ((cc * cf - sc * sf) * scaling).reshape(shape)
    sin_t = ((sc * cf + cc * sf) * scaling).reshape(shape)
    top = jnp.concatenate([cos_t, -sin_t], axis=-1)
    bottom = jnp.concatenate([sin_t, cos_t], axis=-1)
    full = jnp.concatenate([top, bottom], axis=1)
    return split_exact(full)


def split_exact(value):
    scaled = value * 65537.0
    high = scaled - (scaled - value)
    low = value - high
    return high.astype(jnp.bfloat16), low.astype(jnp.bfloat16)


def split_parts(value):
    high = value.astype(jnp.bfloat16)
    low = (value - high.astype(jnp.float32)).astype(jnp.bfloat16)
    return high, low


def spectra_kernel(with_halo, *refs):
    if with_halo:
        xa_ref, fol_ref, sh_ref, wb_ref, bh_ref, bl_ref, _, out_ref, xf_ref, f_ref, uh_ref, ul_ref = refs
    else:
        xa_ref, wb_ref, bh_ref, bl_ref, out_ref, xf_ref, f_ref, uh_ref, ul_ref = refs
    n_in = xa_ref.shape[0]
    own = CHUNK if with_halo else CHUNK + TAPS - 1

    def load_block(q_local, _):
        start = pl.multiple_of(q_local * FFT_LEN, FFT_LEN)
        xf_ref[q_local] = xa_ref[:, pl.ds(start, FFT_LEN)].astype(jnp.float32)
        return 0

    lax.fori_loop(0, own, load_block, 0, unroll=4)

    if with_halo:
        is_final = lax.axis_index("narrow") == lax.axis_size("narrow") - 1

        def body(j, _):
            start = pl.multiple_of(j * FFT_LEN, FFT_LEN)
            lanes = pl.ds(start, FFT_LEN)
            picked = jnp.where(is_final, fol_ref[:, lanes], sh_ref[:, lanes])
            xf_ref[CHUNK + j] = picked.astype(jnp.float32)
            return 0
        lax.fori_loop(0, TAPS - 1, body, 0, unroll=3)

    lane_w = 128
    for lane_at in range(FFT_LEN // lane_w):
        lanes = slice(lane_at * lane_w, (lane_at + 1) * lane_w)
        taps = [wb_ref[p, :, lanes] for p in range(TAPS)]

        def filt(ml, _):
            terms = [taps[p] * xf_ref[ml + p, :, lanes] for p in range(TAPS)]
            while len(terms) > 1:
                terms = [terms[j] + terms[j + 1] for j in range(0, len(terms), 2)]
            f_ref[lane_at, pl.ds(ml, n_in, stride=CHUNK), :] = terms[0]
            return 0

        lax.fori_loop(0, CHUNK, filt, 0, unroll=16)

    half = 1.0 / math.sqrt(2.0)
    rows_per = 16
    sub_rows = 256

    for sub in range((CHUNK * n_in) // sub_rows):

        def butterflies(g, _):
            row = pl.multiple_of(sub * sub_rows + g * rows_per, rows_per)
            local = pl.multiple_of(g * rows_per, rows_per)
            rs = pl.ds(row, rows_per)
            ls = pl.ds(local, rows_per)
            for h in range(2):
                a = [f_ref[2 * n + h, rs, :] for n in range(PHASES)]
                s04 = a[0] + a[4]
                d04 = a[0] - a[4]
                s26 = a[2] + a[6]
                d26 = a[2] - a[6]
                s15 = a[1] + a[5]
                d15 = a[1] - a[5]
                s37 = a[3] + a[7]
                d37 = a[3] - a[7]
                e0 = s04 + s26
                e2 = s04 - s26
                o0 = s15 + s37
                o2 = s15 - s37
                p = half * (d15 - d37)
                q = half * (d15 + d37)
                outs = [
                    (e0 + o0, None),
                    (d04 + p, -d26 - q),
                    (e2, -o2),
                    (d04 - p, d26 - q),
                    (e0 - o0, None),
                    (d04 - p, -d26 + q),
                    (e2, o2),
                    (d04 + p, d26 + q),
                ]
                re_l = slice(h * 128, (h + 1) * 128)
                im_l = slice(SUB_LEN + h * 128, SUB_LEN + (h + 1) * 128)
                for c2, (re, im) in enumerate(outs):
                    hi, lo = split_parts(re)
                    uh_ref[c2, ls, re_l] = hi
                    ul_ref[c2, ls, re_l] = lo
                    if im is not None:
                        hi, lo = split_parts(im)
                        uh_ref[c2, ls, im_l] = hi
                        ul_ref[c2, ls, im_l] = lo
            return 0

        lax.fori_loop(0, sub_rows // rows_per, butterflies, 0, unroll=4)

        for c2 in range(PHASES):
            depth = SUB_LEN if c2 in (0, PHASES // 2) else 2 * SUB_LEN
            uh = uh_ref[c2, :, 0:depth]
            ul = ul_ref[c2, :, 0:depth]
            bh = bh_ref[c2, 0:depth, :]
            bl = bl_ref[c2, 0:depth, :]
            acc = jnp.dot(uh, bh, preferred_element_type=jnp.float32)
            acc = acc + jnp.dot(ul, bh, preferred_element_type=jnp.float32)
            acc = acc + jnp.dot(uh, bl, preferred_element_type=jnp.float32)
            out_ref[0, c2, :, sub * sub_rows:(sub + 1) * sub_rows] = acc.T.astype(jnp.bfloat16)


def pfb_chunk(xa, xh, wb, bh, bl, chunk_at, prev):
    n_in, span = xa.shape
    rows = CHUNK * n_in
    with_halo = xh is not None
    lanes = CHUNK * FFT_LEN if with_halo else (CHUNK + TAPS - 1) * FFT_LEN
    flops = 2 * rows * 3 * SUB_LEN * 2 * SUB_LEN * 7 + 2 * n_in * CHUNK * FFT_LEN * TAPS
    bytes_accessed = n_in * lanes * 2 + PHASES * rows * 2 * SUB_LEN * 2
    xa_spec = pl.BlockSpec((n_in, lanes), lambda s: (0, chunk_at))
    const3 = lambda s: (0, 0, 0)
    in_specs = [pl.BlockSpec(xa_spec.block_shape, xa_spec.index_map, pipeline_mode=pl.Buffered(1))]
    operands = [xa]
    if with_halo:
        for arr in xh:
            in_specs.append(pl.BlockSpec(arr.shape, lambda s: (0, 0), pipeline_mode=pl.Buffered(1)))
            operands.append(arr)
    for arr in (wb, bh, bl):
        in_specs.append(pl.BlockSpec(arr.shape, const3, pipeline_mode=pl.Buffered(1)))
        operands.append(arr)
    aliases = {}
    if with_halo:
        in_specs.append(pl.BlockSpec(memory_space=pl.ANY))
        operands.append(prev)
        aliases = {len(operands) - 1: 0}
    steps = span // FFT_LEN // CHUNK
    return pl.pallas_call(
        functools.partial(spectra_kernel, with_halo),
        out_shape=jax.ShapeDtypeStruct((steps, PHASES, 2 * CHANNELS // PHASES, rows), jnp.bfloat16),
        grid=(1,),
        in_specs=in_specs,
        out_specs=pl.BlockSpec((1, PHASES, 2 * CHANNELS // PHASES, rows), lambda s: (chunk_at, 0, 0, 0)),
        input_output_aliases=aliases,
        scratch_shapes=[
            pltpu.VMEM((CHUNK + TAPS - 1, n_in, FFT_LEN), jnp.float32),
            pltpu.VMEM((FFT_LEN // 128, rows, 128), jnp.float32),
            pltpu.VMEM((PHASES, 256, 2 * SUB_LEN), jnp.bfloat16),
            pltpu.VMEM((PHASES, 256, 2 * SUB_LEN), jnp.bfloat16),
        ],
        compiler_params=pltpu.CompilerParams(
            dimension_semantics=("arbitrary",), vmem_limit_bytes=62 * 1024 * 1024
        ),
        cost_estimate=pl.CostEstimate(flops=flops, transcendentals=0, bytes_accessed=bytes_accessed),
    )(*operands)


def pfb_spectra(xa, xh, wb, bh, bl):
    n_spec = xa.shape[1] // FFT_LEN
    steps = n_spec // CHUNK
    first = pfb_chunk(xa, None, wb, bh, bl, 0, None)
    return pfb_chunk(xa, xh, wb, bh, bl, steps - 1, first)


def gram_kernel(n_narrow, g_ref, out_ref, l_ref):
    n_src = g_ref.shape[0]
    steps = g_ref.shape[3]
    seg = g_ref.shape[5]
    n_in = g_ref.shape[4]

    def gather(w, _):
        row = pl.multiple_of(w * n_in, n_in)
        for n in range(n_narrow):
            for ri in range(2):
                for s in range(steps):
                    col = ((ri * n_narrow + n) * steps + s) * seg
                    l_ref[pl.ds(row, n_in), col:col + seg] = g_ref[w * n_narrow + n, 0, ri, s].astype(jnp.float32)
        return 0

    lax.fori_loop(0, n_src // n_narrow, gather, 0, unroll=4)
    both = l_ref[...].astype(jnp.bfloat16)
    half = both.shape[1] // 2
    turned = jnp.concatenate([both[:, half:], -both[:, :half]], axis=1)
    nt = (((1,), (1,)), ((), ()))
    scale = 1.0 / half
    out_ref[0, 0] = lax.dot_general(both, both, nt, preferred_element_type=jnp.float32) * scale
    out_ref[0, 1] = lax.dot_general(turned, both, nt, preferred_element_type=jnp.float32) * scale


def visibilities(got, n_narrow):
    n_src, phases, parts, steps, n_in, seg = got.shape
    all_inputs = n_src // n_narrow * n_in
    depth = parts * n_narrow * steps * seg
    return pl.pallas_call(
        functools.partial(gram_kernel, n_narrow),
        out_shape=jax.ShapeDtypeStruct((phases, 2, all_inputs, all_inputs), jnp.float32),
        grid=(phases,),
        in_specs=[pl.BlockSpec((n_src, 1, parts, steps, n_in, seg), lambda c: (0, c, 0, 0, 0, 0))],
        out_specs=pl.BlockSpec((1, 2, all_inputs, all_inputs), lambda c: (c, 0, 0, 0)),
        scratch_shapes=[pltpu.VMEM((all_inputs, depth), jnp.float32)],
        compiler_params=pltpu.CompilerParams(
            dimension_semantics=("arbitrary",), vmem_limit_bytes=48 * 1024 * 1024
        ),
        cost_estimate=pl.CostEstimate(
            flops=phases * 4 * all_inputs * all_inputs * depth,
            transcendentals=0,
            bytes_accessed=got.size * 2 + phases * 2 * all_inputs * all_inputs * 4,
        ),
    )(got)


def shards(voltages, following):
    local_inputs, local_span = voltages.shape
    local_spec = local_span // FFT_LEN
    halo_len = (TAPS - 1) * FFT_LEN
    leading = voltages[:, :halo_len]
    shifted = from_behind(leading, "narrow", -1)
    after_rows = (following, shifted)
    weights_taps = pfb_window(FFT_LEN, TAPS).reshape(TAPS, 1, FFT_LEN)
    wb = jnp.broadcast_to(weights_taps, (TAPS, local_inputs, FFT_LEN))
    salt = lax.optimization_barrier(jnp.zeros((), jnp.int32))
    bh, bl = phase_matrices(salt)
    out = pfb_spectra(voltages, after_rows, wb, bh, bl)
    steps = local_spec // CHUNK
    c1_len = CHANNELS // PHASES
    out = out.reshape(steps, PHASES, 2, c1_len, local_inputs, CHUNK)
    spec = jnp.transpose(out, (3, 1, 2, 0, 4, 5))
    got = lax.all_to_all(spec, ("wide", "narrow"), 0, 0, tiled=True)
    return visibilities(got, lax.axis_size("narrow"))


def solution(mesh):
    in_specs = (P("wide", "narrow"), P("wide", None))
    out_specs = P(("wide", "narrow"), None, None, None)
    return jax.shard_map(shards, mesh=mesh, in_specs=in_specs, out_specs=out_specs, check_vma=False)
```
